256 devices in a mesh: dp: 32 (over x, z), seq: 8 (over y, core).
Axes of the slice: x: 4, y: 4, z: 8, core: 2. Of those that a mesh axis runs over, the one named last changes fastest.
Arguments:
- xbc: bfloat16 [32, 2048, 2816], P('dp', 'seq'), may hold values from -6 to 6
- gate_input: bfloat16 [32, 2048, 2560], P('dp', 'seq'), may hold values from -6 to 6
- dt_raw: bfloat16 [32, 2048, 40], P('dp', 'seq'), may hold values from -3 to 3
- conv_weight: float32 [4, 2816], replicated, may hold values from -3 to 3
- conv_bias: float32 [2816], replicated, may hold values from -3 to 3
- dt_bias: float32 [40], replicated, may hold values from -0.5 to 0.5
- a_rate: float32 [40], replicated, may hold values from 9.765625e-05 to 0.05
- d_skip: float32 [40], replicated, may hold values from 0.5 to 1.5
- norm_gain: float32 [2560], replicated, may hold values from 0.25 to 1.75
- labels: int32 [32], P('dp'), may hold values from 0 to 1, as said below
- readout: int32 [32, 4], P('dp'), may hold values from 0 to 2047
Outputs:
- layer_out: bfloat16 [32, 2048, 2560], P('dp', 'seq')
- steering: float32 [2560, 128], P(('dp', 'seq'))
The draws below stay inside these ranges and needn't reach their ends.
Inputs may be any that keep to these rules, and one draw needn't show every extreme that they name: `labels`: every label is 0 or 1, and both classes occur.
All inputs are finite; a program needn't handle non-finite values.
Results may differ from the reference program's by a relative error of at most 0.0034.
Values may be sent and summed in bfloat16 or wider, within the bound.
A program may use at most 64 MiB of HBM per device.

```python
import math
import jax
import jax.numpy as jnp
from jax import lax

H = 40
P_SIZE = 64
N = 128
KW = 4
R = 4
L_DEV = 256
CH = 2816
BATCH = 32
SEQLEN = 2048


def draw_labels(key, part):
    values = jax.random.randint(key, (BATCH,), 0, 2, dtype=jnp.int32)
    return values.at[0].set(0).at[1].set(1)


def set_ends(array, key, low, largest):
    dims = array.shape
    spot = [jax.random.randint(jax.random.fold_in(key, axis), (), 0, dims[axis]) for axis in range(len(dims))]
    array = array.at[tuple(spot)].set(low)
    longest = dims.index(max(dims))
    spot[longest] = (spot[longest] + 1) % dims[longest]
    return array.at[tuple(spot)].set(largest)


def steps_of(key, shape, split, low, high):
    loudness = 1.0
    for position, shards_of in split:
        draws = jax.random.uniform(jax.random.fold_in(jax.random.fold_in(key, 6), position), (shards_of,), jnp.float32, low / len(split), high / len(split))
        loudness = loudness * jnp.repeat(jnp.exp(draws), shape[position] // shards_of).reshape((-1,) + (1,) * (len(shape) - 1 - position))
    return loudness


def noise(stream_key, shape, scale, bound, shards=(), kind=jnp.bfloat16):
    entries = jax.random.normal(stream_key, shape, jnp.float32) * scale
    if len(shards) > 0:
        entries = steps_of(stream_key, shape, shards, -0.22, 0.18) * entries
    return jnp.clip(entries, min=-bound, max=bound).astype(kind)


def setup_inputs(seed: int = 0) -> dict:
    seeds = jax.random.split(jax.random.key(seed), 12)
    xbc = noise(seeds[0], (BATCH, SEQLEN, CH), 1.0, 6.0, ((0, 32), (1, 8)))
    gate_input = noise(seeds[1], (BATCH, SEQLEN, H * P_SIZE), 1.0, 6.0, ((0, 32), (1, 8)))
    dt_raw = noise(seeds[2], (BATCH, SEQLEN, H), 0.5, 3.0, ((0, 32), (1, 8)))
    conv_weight = noise(seeds[3], (KW, CH), KW ** -0.5, 3.0, (), jnp.float32)
    conv_bias = noise(seeds[4], (CH,), 0.5, 3.0, (), jnp.float32)
    dt_bias = jnp.clip(jax.random.uniform(seeds[5], (H,), jnp.float32, -0.5, 0.5), -0.5, 0.5)
    a_rate = jnp.clip(jnp.exp(jax.random.uniform(seeds[6], (H,), jnp.float32, math.log(9.765625145519152e-05), math.log(0.05))), 9.765625145519152e-05, 0.05)
    d_skip = jnp.clip(jax.random.uniform(seeds[7], (H,), jnp.float32, 0.5, 1.5), 0.5, 1.5)
    norm_gain = jnp.clip(1.0 + 0.15 * jax.random.normal(seeds[8], (H * P_SIZE,), jnp.float32), 0.25, 1.75)
    labels = draw_labels(jax.random.fold_in(seeds[11], 71), 0)
    readout = set_ends(jax.random.randint(seeds[10], (BATCH, R), 0, SEQLEN), jax.random.fold_in(seeds[10], 1), 0, SEQLEN - 1).astype(jnp.int32)
    return {"xbc": xbc, "gate_input": gate_input, "dt_raw": dt_raw, "conv_weight": conv_weight, "conv_bias": conv_bias, "dt_bias": dt_bias, "a_rate": a_rate, "d_skip": d_skip, "norm_gain": norm_gain, "labels": labels, "readout": readout}


group_heads = 8
highest = lax.Precision.HIGHEST

def local_terms(x_vals, b_vals, c_vals, dt_vals, cumulative, points, offset):
    row_count = x_vals.shape[0]
    x_wide = x_vals.astype(jnp.float32).reshape(row_count, H, P_SIZE)
    b_wide = b_vals.astype(jnp.float32)
    c_wide = c_vals.astype(jnp.float32)
    scores = lax.dot_general(c_vals, b_vals, (((1,), (1,)), ((), ())), preferred_element_type=jnp.float32)
    positions = jnp.arange(row_count, dtype=jnp.int32)
    causal = positions[:, None] >= positions[None, :]
    cum_heads = cumulative.T
    dt_heads = dt_vals.T

    def group_step(group_index, buffer):
        head_start = group_index * group_heads
        cum_group = lax.dynamic_slice_in_dim(cum_heads, head_start, group_heads, 0)
        dt_group = lax.dynamic_slice_in_dim(dt_heads, head_start, group_heads, 0)
        x_group = lax.dynamic_slice_in_dim(x_wide, head_start, group_heads, 1)
        spread = jnp.where(causal[None], cum_group[:, :, None] - cum_group[:, None, :], -1e+30)
        weight = jnp.exp(spread) * dt_group[:, None, :] * scores[None]
        partial_value = jnp.einsum('hts,shp->thp', weight, x_group, precision=highest)
        return lax.dynamic_update_slice_in_dim(buffer, partial_value, head_start, 1)
    diagonal_part = lax.fori_loop(0, H // group_heads, group_step, jnp.zeros((row_count, H, P_SIZE), jnp.float32))
    final_log = cumulative[row_count - 1]
    to_end = jnp.exp(final_log[None, :] - cumulative) * dt_vals
    decay_total = jnp.exp(final_log)
    local_state = jnp.einsum('sk,sn->kn', (to_end[:, :, None] * x_wide).reshape(row_count, H * P_SIZE), b_wide, precision=highest).reshape(H, P_SIZE, N)
    local_index = (points - offset).astype(jnp.int32)
    owned_flag = ((local_index >= 0) & (local_index < row_count)).astype(jnp.float32)
    one_hot = (positions[None, :] == local_index[:, None]).astype(jnp.float32)
    cum_at = jnp.dot(one_hot, cumulative, precision=highest)
    before = positions[None, :] <= local_index[:, None]
    spread = jnp.where(before[:, :, None], cum_at[:, None, :] - cumulative[None], -1e+30)
    read_weight = lax.optimization_barrier(jnp.sum(owned_flag[:, None, None] * jnp.exp(spread), axis=0)) * dt_vals / R
    carry_weight = lax.optimization_barrier(jnp.sum(owned_flag[:, None] * jnp.exp(cum_at), axis=0)) / R
    read_local = jnp.einsum('sk,sn->kn', (read_weight[:, :, None] * x_wide).reshape(row_count, H * P_SIZE), b_wide, precision=highest).reshape(H, P_SIZE, N)
    return (diagonal_part, x_wide, c_wide, local_state, decay_total, read_local, carry_weight)

def finish_block(diagonal_part, x_wide, c_wide, cumulative, h_in, gate_rows, d_skip, norm_gain):
    row_count = x_wide.shape[0]
    incoming = jnp.einsum('tn,hpn->thp', c_wide, h_in, precision=highest)
    ssm_out = diagonal_part + jnp.exp(cumulative)[:, :, None] * incoming + d_skip[None, :, None] * x_wide
    gated_out = ssm_out.reshape(row_count, H * P_SIZE) * jax.nn.silu(gate_rows.astype(jnp.float32))
    inv_rms = lax.rsqrt(lax.optimization_barrier(jnp.mean(gated_out * gated_out, axis=-1, keepdims=True)) + 1e-05)
    return (gated_out * inv_rms * norm_gain).astype(jnp.bfloat16)

def reference(xbc, gate_input, dt_raw, conv_weight, conv_bias, dt_bias, a_rate, d_skip, norm_gain, labels, readout):
    n_one = jnp.sum(labels.astype(jnp.float32))
    n_zero = labels.shape[0] - n_one
    blocks = SEQLEN // L_DEV

    def one_sequence(sequence):
        seq_rows, gate_rows, raw_rows, class_label, points = sequence
        padded = jnp.concatenate([jnp.zeros((KW - 1, CH), jnp.bfloat16), seq_rows], axis=0).astype(jnp.float32)
        conv_sum = conv_bias
        for tap_index in range(KW):
            conv_sum = conv_sum + conv_weight[tap_index] * padded[tap_index:tap_index + SEQLEN]
        activated = jax.nn.silu(conv_sum).astype(jnp.bfloat16)
        dt_vals = jax.nn.softplus(raw_rows.astype(jnp.float32) + dt_bias)

        def block_step(scan_carry, block_in):
            carried, mean_state = scan_carry
            act_block, gate_block, dt_block, block_index = block_in
            cumulative = jnp.cumsum(-a_rate * dt_block, axis=0)
            diagonal_part, x_wide, c_wide, local_state, decay_total, read_local, carry_weight = local_terms(act_block[:, :H * P_SIZE], act_block[:, H * P_SIZE:H * P_SIZE + N], act_block[:, H * P_SIZE + N:], dt_block, cumulative, points, block_index * L_DEV)
            outputs = finish_block(diagonal_part, x_wide, c_wide, cumulative, carried, gate_block, d_skip, norm_gain)
            mean_state = mean_state + carry_weight[:, None, None] * carried + read_local
            carried = decay_total[:, None, None] * carried + local_state
            return ((carried, mean_state), outputs)
        start_state = jnp.zeros((H, P_SIZE, N), jnp.float32)
        block_ids = jnp.arange(blocks).astype(jnp.int32)
        (carried, mean_state), outputs = lax.scan(block_step, (start_state, start_state), (activated.reshape(blocks, L_DEV, CH), gate_rows.reshape(blocks, L_DEV, H * P_SIZE), dt_vals.reshape(blocks, L_DEV, H), block_ids))
        class_value = class_label.astype(jnp.float32)
        class_weight = class_value / n_one - (1.0 - class_value) / n_zero
        return (outputs.reshape(SEQLEN, H * P_SIZE), class_weight * mean_state)
    layer_out, partials = lax.map(one_sequence, (xbc, gate_input, dt_raw, labels, readout))
    return (layer_out, lax.optimization_barrier(jnp.sum(partials, axis=0)).reshape(H * P_SIZE, N))
```

```python
import jax
import jax.numpy as jnp
from jax import lax
from jax.sharding import PartitionSpec as P

H = 40
P_SIZE = 64
N = 128
KW = 4
R = 4


group_heads = 8
highest = lax.Precision.HIGHEST


def from_behind(block, axis, distance):
    devices = range(lax.axis_size(axis))
    route = [(i - distance, i) for i in devices if i - distance in devices]
    return lax.ppermute(block, axis, route)


def local_terms(x_vals, b_vals, c_vals, dt_vals, cumulative, points, offset):
    row_count = x_vals.shape[0]
    x_wide = x_vals.astype(jnp.float32).reshape(row_count, H, P_SIZE)
    b_wide = b_vals.astype(jnp.float32)
    c_wide = c_vals.astype(jnp.float32)
    scores = lax.dot_general(
        c_vals, b_vals, (((1,), (1,)), ((), ())), preferred_element_type=jnp.float32
    )
    positions = jnp.arange(row_count, dtype=jnp.int32)
    causal = positions[:, None] >= positions[None, :]
    cum_heads = cumulative.T
    dt_heads = dt_vals.T

    def group_step(group_index, buffer):
        head_start = group_index * group_heads
        cum_group = lax.dynamic_slice_in_dim(cum_heads, head_start, group_heads, 0)
        dt_group = lax.dynamic_slice_in_dim(dt_heads, head_start, group_heads, 0)
        x_group = lax.dynamic_slice_in_dim(x_wide, head_start, group_heads, 1)
        spread = jnp.where(causal[None], cum_group[:, :, None] - cum_group[:, None, :], -1e30)
        weight = jnp.exp(spread) * dt_group[:, None, :] * scores[None]
        partial_value = jnp.einsum("hts,shp->thp", weight, x_group, precision=highest)
        return lax.dynamic_update_slice_in_dim(buffer, partial_value, head_start, 1)

    diagonal_part = lax.fori_loop(
        0, H // group_heads, group_step, jnp.zeros((row_count, H, P_SIZE), jnp.float32)
    )
    final_log = cumulative[row_count - 1]
    to_end = jnp.exp(final_log[None, :] - cumulative) * dt_vals
    decay_total = jnp.exp(final_log)
    local_state = jnp.einsum(
        "sk,sn->kn",
        (to_end[:, :, None] * x_wide).reshape(row_count, H * P_SIZE),
        b_wide,
        precision=highest,
    ).reshape(H, P_SIZE, N)
    local_index = points - offset
    owned_flag = ((local_index >= 0) & (local_index < row_count)).astype(jnp.float32)
    one_hot = (positions[None, :] == local_index[:, None]).astype(jnp.float32)
    cum_at = jnp.dot(one_hot, cumulative, precision=highest)
    before = positions[None, :] <= local_index[:, None]
    spread = jnp.where(before[:, :, None], cum_at[:, None, :] - cumulative[None], -1e30)
    read_weight = jnp.sum(owned_flag[:, None, None] * jnp.exp(spread), axis=0) * dt_vals / R
    carry_weight = jnp.sum(owned_flag[:, None] * jnp.exp(cum_at), axis=0) / R
    return (
        diagonal_part, x_wide, b_wide, c_wide, local_state, decay_total, to_end, read_weight, carry_weight
    )


def finish_block(diagonal_part, x_wide, c_wide, cumulative, h_in, gate_rows, d_skip, norm_gain):
    row_count = x_wide.shape[0]
    incoming = jnp.einsum("tn,hpn->thp", c_wide, h_in, precision=highest)
    ssm_out = (
        diagonal_part + jnp.exp(cumulative)[:, :, None] * incoming + d_skip[None, :, None] * x_wide
    )
    gated_out = ssm_out.reshape(row_count, H * P_SIZE) * jax.nn.silu(gate_rows.astype(jnp.float32))
    inv_rms = lax.rsqrt(jnp.mean(gated_out * gated_out, axis=-1, keepdims=True) + 1e-05)
    return (gated_out * inv_rms * norm_gain).astype(jnp.bfloat16)


def on_device(
    xbc,
    gate_input,
    dt_raw,
    conv_weight,
    conv_bias,
    dt_bias,
    a_rate,
    d_skip,
    norm_gain,
    labels,
    readout,
):
    row_count = xbc.shape[1]
    seq_count = lax.axis_size("seq")
    me = lax.axis_index("seq")
    n_one = jnp.sum(lax.all_gather(labels, "dp", tiled=True).astype(jnp.float32))
    edge_rows = from_behind(xbc[:, row_count - (KW - 1) :, :], "seq", 1)
    padded = jnp.concatenate([edge_rows, xbc], axis=1)[0].astype(jnp.float32)
    conv_sum = conv_bias
    for tap_index in range(KW):
        conv_sum = conv_sum + conv_weight[tap_index] * padded[tap_index : tap_index + row_count]
    activated = jax.nn.silu(conv_sum).astype(jnp.bfloat16)
    dt_vals = jax.nn.softplus(dt_raw[0].astype(jnp.float32) + dt_bias)
    cumulative = jnp.cumsum(-a_rate * dt_vals, axis=0)
    offset = me * row_count
    (diagonal_part, x_wide, b_wide, c_wide, local_state, decay_total, to_end, read_weight,
     carry_weight) = local_terms(
        activated[:, : H * P_SIZE],
        activated[:, H * P_SIZE : H * P_SIZE + N],
        activated[:, H * P_SIZE + N :],
        dt_vals,
        cumulative,
        readout[0],
        offset,
    )
    scalars = lax.all_gather(jnp.stack([decay_total, carry_weight]), "seq")
    coef_rows = [jnp.zeros_like(decay_total)]
    for later in range(seq_count - 1, 0, -1):
        coef_rows.append(scalars[later, 1] + scalars[later, 0] * coef_rows[-1])
    coef_all = jnp.stack(coef_rows[::-1])
    coef = jnp.sum(jnp.where((jnp.arange(seq_count) == me)[:, None], coef_all, 0.0), axis=0)
    mean_weight = coef[None, :] * to_end + read_weight
    mean_local = jnp.einsum(
        "sk,sn->kn",
        (mean_weight[:, :, None] * x_wide).reshape(row_count, H * P_SIZE),
        b_wide,
        precision=highest,
    )
    batch_count = lax.axis_size("dp")
    class_value = labels[0].astype(jnp.float32)
    class_weight = class_value / n_one - (1.0 - class_value) / (batch_count - n_one)
    partial_value = class_weight * mean_local
    steering = lax.psum_scatter(partial_value, "dp", scatter_dimension=0, tiled=True)
    steering = lax.psum_scatter(steering, "seq", scatter_dimension=0, tiled=True)
    h_in = jnp.zeros((H, P_SIZE, N), jnp.float32)
    for step_index in range(seq_count - 1):
        h_in = from_behind(decay_total[:, None, None] * h_in + local_state, "seq", 1)
    layer_out = finish_block(
        diagonal_part, x_wide, c_wide, cumulative, h_in, gate_input[0], d_skip, norm_gain
    )
    return (layer_out[None], steering)


def solution(mesh):
    return jax.shard_map(
        on_device,
        mesh=mesh,
        in_specs=(
            P("dp", "seq", None),
            P("dp", "seq", None),
            P("dp", "seq", None),
            P(),
            P(),
            P(),
            P(),
            P(),
            P(),
            P("dp"),
            P("dp", None),
        ),
        out_specs=(P("dp", "seq", None), P(("dp", "seq"), None)),
        check_vma=False,
    )
```

```python
import jax
import jax.numpy as jnp
from jax import lax
from jax.sharding import PartitionSpec as P
from jax.experimental import pallas as pl
from jax.experimental.pallas import tpu as pltpu
import functools

H = 40
P_SIZE = 64
N = 128
KW = 4
R = 4


MESH_ID = pl.DeviceIdType.MESH


def _halving_plan(dp_count, seq_count):
    plan = []
    bit = 1
    while bit < seq_count:
        plan.append(("seq", bit))
        bit *= 2
    bit = 1
    while bit < dp_count:
        plan.append(("dp", bit))
        bit *= 2
    return plan


def _reduce_scatter_kernel(plan, in_ref, out_ref, acc, *rest):
    rounds = len(plan)
    recv = rest[:rounds]
    send_sem, recv_sem = rest[rounds], rest[rounds + 1]
    coords = {"dp": lax.axis_index("dp"), "seq": lax.axis_index("seq")}

    def partner_of(axis, bit):
        me = coords[axis]
        return me + bit - 2 * bit * ((me // bit) % 2)

    def device_of(axis, bit):
        if axis == "dp":
            return (partner_of(axis, bit), coords["seq"])
        return (coords["dp"], partner_of(axis, bit))

    barrier = pltpu.get_barrier_semaphore()
    for axis, bit in plan:
        pl.semaphore_signal(barrier, inc=1, device_id=device_of(axis, bit), device_id_type=MESH_ID)
    pl.semaphore_wait(barrier, rounds)

    size = in_ref.shape[0]
    base = 0
    copies = []
    for index, (axis, bit) in enumerate(plan):
        half = size // 2
        mine = (coords[axis] // bit) % 2
        keep = base + mine * half
        give = base + (1 - mine) * half
        source = in_ref if index == 0 else acc
        copy = pltpu.make_async_remote_copy(
            src_ref=source.at[pl.ds(give, half)],
            dst_ref=recv[index],
            send_sem=send_sem.at[index],
            recv_sem=recv_sem.at[index],
            device_id=device_of(axis, bit),
            device_id_type=MESH_ID,
        )
        copy.start()
        copy.wait_recv()
        acc[pl.ds(keep, half)] = source[pl.ds(keep, half)] + recv[index][...]
        copies.append(copy)
        base = keep
        size = half
    out_ref[...] = acc[pl.ds(base, 1)]
    for copy in copies:
        copy.wait_send()


def reduce_scatter_blocks(blocks):
    dp_count = lax.axis_size("dp")
    seq_count = lax.axis_size("seq")
    plan = _halving_plan(dp_count, seq_count)
    n_blocks, rows, cols = blocks.shape
    recv_shapes = [pltpu.VMEM((n_blocks >> (i + 1), rows, cols), blocks.dtype) for i in range(len(plan))]
    return pl.pallas_call(
        functools.partial(_reduce_scatter_kernel, plan),
        out_shape=jax.ShapeDtypeStruct((1, rows, cols), blocks.dtype),
        in_specs=[pl.BlockSpec(memory_space=pltpu.VMEM)],
        out_specs=pl.BlockSpec(memory_space=pltpu.VMEM),
        scratch_shapes=[pltpu.VMEM((n_blocks, rows, cols), blocks.dtype)] + recv_shapes + [
            pltpu.SemaphoreType.DMA((len(plan),)),
            pltpu.SemaphoreType.DMA((len(plan),)),
        ],
        compiler_params=pltpu.CompilerParams(collective_id=1, has_side_effects=True),
    )(blocks)


def to_halving_order(partial, dp_count, seq_count, rows):
    total_bits = (dp_count * seq_count).bit_length() - 1
    cols = partial.shape[-1]
    view = partial.reshape((2,) * total_bits + (rows, cols))
    order = tuple(range(total_bits - 1, -1, -1)) + (total_bits, total_bits + 1)
    return view.transpose(order).reshape(dp_count * seq_count, rows, cols)


group_heads = 8
highest = lax.Precision.HIGHEST


def from_behind(block, axis, distance):
    devices = range(lax.axis_size(axis))
    route = [(i - distance, i) for i in devices if i - distance in devices]
    return lax.ppermute(block, axis, route)


def local_terms(x_vals, b_vals, c_vals, dt_vals, cumulative, points, offset):
    row_count = x_vals.shape[0]
    x_wide = x_vals.astype(jnp.float32).reshape(row_count, H, P_SIZE)
    b_wide = b_vals.astype(jnp.float32)
    c_wide = c_vals.astype(jnp.float32)
    scores = lax.dot_general(
        c_vals, b_vals, (((1,), (1,)), ((), ())), preferred_element_type=jnp.float32
    )
    positions = jnp.arange(row_count, dtype=jnp.int32)
    causal = positions[:, None] >= positions[None, :]
    cum_heads = cumulative.T
    dt_heads = dt_vals.T

    def group_step(group_index, buffer):
        head_start = group_index * group_heads
        cum_group = lax.dynamic_slice_in_dim(cum_heads, head_start, group_heads, 0)
        dt_group = lax.dynamic_slice_in_dim(dt_heads, head_start, group_heads, 0)
        x_group = lax.dynamic_slice_in_dim(x_wide, head_start, group_heads, 1)
        spread = jnp.where(causal[None], cum_group[:, :, None] - cum_group[:, None, :], -1e30)
        weight = jnp.exp(spread) * dt_group[:, None, :] * scores[None]
        partial_value = jnp.einsum("hts,shp->thp", weight, x_group, precision=highest)
        return lax.dynamic_update_slice_in_dim(buffer, partial_value, head_start, 1)

    diagonal_part = lax.fori_loop(
        0, H // group_heads, group_step, jnp.zeros((row_count, H, P_SIZE), jnp.float32)
    )
    final_log = cumulative[row_count - 1]
    to_end = jnp.exp(final_log[None, :] - cumulative) * dt_vals
    decay_total = jnp.exp(final_log)
    local_state = jnp.einsum(
        "sk,sn->kn",
        (to_end[:, :, None] * x_wide).reshape(row_count, H * P_SIZE),
        b_wide,
        precision=highest,
    ).reshape(H, P_SIZE, N)
    local_index = points - offset
    owned_flag = ((local_index >= 0) & (local_index < row_count)).astype(jnp.float32)
    one_hot = (positions[None, :] == local_index[:, None]).astype(jnp.float32)
    cum_at = jnp.dot(one_hot, cumulative, precision=highest)
    before = positions[None, :] <= local_index[:, None]
    spread = jnp.where(before[:, :, None], cum_at[:, None, :] - cumulative[None], -1e30)
    read_weight = jnp.sum(owned_flag[:, None, None] * jnp.exp(spread), axis=0) * dt_vals / R
    carry_weight = jnp.sum(owned_flag[:, None] * jnp.exp(cum_at), axis=0) / R
    return (
        diagonal_part, x_wide, b_wide, c_wide, local_state, decay_total, to_end, read_weight, carry_weight
    )


def finish_block(diagonal_part, x_wide, c_wide, cumulative, h_in, gate_rows, d_skip, norm_gain):
    row_count = x_wide.shape[0]
    incoming = jnp.einsum("tn,hpn->thp", c_wide, h_in, precision=highest)
    ssm_out = (
        diagonal_part + jnp.exp(cumulative)[:, :, None] * incoming + d_skip[None, :, None] * x_wide
    )
    gated_out = ssm_out.reshape(row_count, H * P_SIZE) * jax.nn.silu(gate_rows.astype(jnp.float32))
    inv_rms = lax.rsqrt(jnp.mean(gated_out * gated_out, axis=-1, keepdims=True) + 1e-05)
    return (gated_out * inv_rms * norm_gain).astype(jnp.bfloat16)


def on_device(
    xbc,
    gate_input,
    dt_raw,
    conv_weight,
    conv_bias,
    dt_bias,
    a_rate,
    d_skip,
    norm_gain,
    labels,
    readout,
):
    row_count = xbc.shape[1]
    seq_count = lax.axis_size("seq")
    me = lax.axis_index("seq")
    n_one = jnp.sum(lax.all_gather(labels, "dp", tiled=True).astype(jnp.float32))
    edge_rows = from_behind(xbc[:, row_count - (KW - 1) :, :], "seq", 1)
    padded = jnp.concatenate([edge_rows, xbc], axis=1)[0].astype(jnp.float32)
    conv_sum = conv_bias
    for tap_index in range(KW):
        conv_sum = conv_sum + conv_weight[tap_index] * padded[tap_index : tap_index + row_count]
    activated = jax.nn.silu(conv_sum).astype(jnp.bfloat16)
    dt_vals = jax.nn.softplus(dt_raw[0].astype(jnp.float32) + dt_bias)
    cumulative = jnp.cumsum(-a_rate * dt_vals, axis=0)
    offset = me * row_count
    (diagonal_part, x_wide, b_wide, c_wide, local_state, decay_total, to_end, read_weight,
     carry_weight) = local_terms(
        activated[:, : H * P_SIZE],
        activated[:, H * P_SIZE : H * P_SIZE + N],
        activated[:, H * P_SIZE + N :],
        dt_vals,
        cumulative,
        readout[0],
        offset,
    )
    scalars = lax.all_gather(jnp.stack([decay_total, carry_weight]), "seq")
    coef_rows = [jnp.zeros_like(decay_total)]
    for later in range(seq_count - 1, 0, -1):
        coef_rows.append(scalars[later, 1] + scalars[later, 0] * coef_rows[-1])
    coef_all = jnp.stack(coef_rows[::-1])
    coef = jnp.sum(jnp.where((jnp.arange(seq_count) == me)[:, None], coef_all, 0.0), axis=0)
    mean_weight = coef[None, :] * to_end + read_weight
    mean_local = jnp.einsum(
        "sk,sn->kn",
        (mean_weight[:, :, None] * x_wide).reshape(row_count, H * P_SIZE),
        b_wide,
        precision=highest,
    )
    batch_count = lax.axis_size("dp")
    class_value = labels[0].astype(jnp.float32)
    class_weight = class_value / n_one - (1.0 - class_value) / (batch_count - n_one)
    partial_value = class_weight * mean_local
    block_rows = partial_value.shape[0] // (batch_count * seq_count)
    blocks = to_halving_order(partial_value, batch_count, seq_count, block_rows)
    steering = reduce_scatter_blocks(blocks)[0]
    h_in = jnp.zeros((H, P_SIZE, N), jnp.float32)
    for step_index in range(seq_count - 1):
        h_in = from_behind(decay_total[:, None, None] * h_in + local_state, "seq", 1)
    layer_out = finish_block(
        diagonal_part, x_wide, c_wide, cumulative, h_in, gate_input[0], d_skip, norm_gain
    )
    return (layer_out[None], steering)


def solution(mesh):
    return jax.shard_map(
        on_device,
        mesh=mesh,
        in_specs=(
            P("dp", "seq", None),
            P("dp", "seq", None),
            P("dp", "seq", None),
            P(),
            P(),
            P(),
            P(),
            P(),
            P(),
            P("dp"),
            P("dp", None),
        ),
        out_specs=(P("dp", "seq", None), P(("dp", "seq"), None)),
        check_vma=False,
    )
```

```python
import jax
import jax.numpy as jnp
from jax import lax
from jax.sharding import PartitionSpec as P
from jax.experimental import pallas as pl
from jax.experimental.pallas import tpu as pltpu
import functools

H = 40
P_SIZE = 64
N = 128
KW = 4
R = 4


MESH_ID = pl.DeviceIdType.MESH


def _halving_plan(dp_count, seq_count):
    plan = []
    bit = 1
    while bit < seq_count:
        plan.append(("seq", bit))
        bit *= 2
    bit = 1
    while bit < dp_count:
        plan.append(("dp", bit))
        bit *= 2
    return plan


def _reduce_scatter_kernel(plan, in_ref, out_ref, acc, *rest):
    rounds = len(plan)
    recv = rest[:rounds]
    send_sem, recv_sem = rest[rounds], rest[rounds + 1]
    coords = {"dp": lax.axis_index("dp"), "seq": lax.axis_index("seq")}

    def partner_of(axis, bit):
        me = coords[axis]
        return me + bit - 2 * bit * ((me // bit) % 2)

    def device_of(axis, bit):
        if axis == "dp":
            return (partner_of(axis, bit), coords["seq"])
        return (coords["dp"], partner_of(axis, bit))

    barrier = pltpu.get_barrier_semaphore()
    for axis, bit in plan:
        pl.semaphore_signal(barrier, inc=1, device_id=device_of(axis, bit), device_id_type=MESH_ID)
    pl.semaphore_wait(barrier, rounds)

    size = in_ref.shape[0]
    base = 0
    copies = []
    for index, (axis, bit) in enumerate(plan):
        half = size // 2
        mine = (coords[axis] // bit) % 2
        keep = base + mine * half
        give = base + (1 - mine) * half
        source = in_ref if index == 0 else acc
        copy = pltpu.make_async_remote_copy(
            src_ref=source.at[pl.ds(give, half)],
            dst_ref=recv[index],
            send_sem=send_sem.at[index],
            recv_sem=recv_sem.at[index],
            device_id=device_of(axis, bit),
            device_id_type=MESH_ID,
        )
        copy.start()
        copy.wait_recv()
        acc[pl.ds(keep, half)] = source[pl.ds(keep, half)] + recv[index][...]
        copies.append(copy)
        base = keep
        size = half
    out_ref[...] = acc[pl.ds(base, 1)]
    for copy in copies:
        copy.wait_send()


def reduce_scatter_blocks(blocks):
    dp_count = lax.axis_size("dp")
    seq_count = lax.axis_size("seq")
    plan = _halving_plan(dp_count, seq_count)
    n_blocks, rows, cols = blocks.shape
    recv_shapes = [pltpu.VMEM((n_blocks >> (i + 1), rows, cols), blocks.dtype) for i in range(len(plan))]
    return pl.pallas_call(
        functools.partial(_reduce_scatter_kernel, plan),
        out_shape=jax.ShapeDtypeStruct((1, rows, cols), blocks.dtype),
        in_specs=[pl.BlockSpec(memory_space=pltpu.VMEM)],
        out_specs=pl.BlockSpec(memory_space=pltpu.VMEM),
        scratch_shapes=[pltpu.VMEM((n_blocks, rows, cols), blocks.dtype)] + recv_shapes + [
            pltpu.SemaphoreType.DMA((len(plan),)),
            pltpu.SemaphoreType.DMA((len(plan),)),
        ],
        compiler_params=pltpu.CompilerParams(collective_id=1, has_side_effects=True),
    )(blocks)


def to_halving_order(partial, dp_count, seq_count, rows):
    total_bits = (dp_count * seq_count).bit_length() - 1
    cols = partial.shape[-1]
    view = partial.reshape((2,) * total_bits + (rows, cols))
    order = tuple(range(total_bits - 1, -1, -1)) + (total_bits, total_bits + 1)
    return view.transpose(order).reshape(dp_count * seq_count, rows, cols)


def _chain_kernel(chunk, local_ref, decay_ref, hin_ref, send_buf, send_sem, recv_sem):
    count = lax.axis_size("seq")
    me = lax.axis_index("seq")
    row_id = lax.axis_index("dp")
    has_left = (me + count - 1) // count
    has_right = (2 * count - 2 - me) // count
    left = me - has_left
    right = me + has_right
    pieces = local_ref.shape[0] // chunk

    barrier = pltpu.get_barrier_semaphore()

    @pl.when(has_left == 1)
    def _():
        pl.semaphore_signal(barrier, inc=1, device_id=(row_id, left), device_id_type=MESH_ID)

    @pl.when(has_right == 1)
    def _():
        pl.semaphore_signal(barrier, inc=1, device_id=(row_id, right), device_id_type=MESH_ID)

    pl.semaphore_wait(barrier, has_left + has_right)

    def link(source, piece):
        rows = pl.ds(piece * chunk, chunk)
        return pltpu.make_async_remote_copy(
            src_ref=source.at[rows],
            dst_ref=hin_ref.at[rows],
            send_sem=send_sem.at[piece],
            recv_sem=recv_sem.at[piece],
            device_id=(row_id, right),
            device_id_type=MESH_ID,
        )

    @pl.when(has_left == 0)
    def _():
        hin_ref[...] = jnp.zeros_like(hin_ref)
        for piece in range(pieces):
            link(local_ref, piece).start()

    @pl.when(has_left == 1)
    def _():
        for piece in range(pieces):
            rows = pl.ds(piece * chunk, chunk)
            link(send_buf, piece).wait_recv()

            @pl.when(has_right == 1)
            def _():
                send_buf[rows] = decay_ref[rows] * hin_ref[rows] + local_ref[rows]
                link(send_buf, piece).start()

    @pl.when(has_right == 1)
    def _():
        for piece in range(pieces):
            link(send_buf, piece).wait_send()


def carry_chain(local_state, decay_total, pieces=8):
    heads = local_state.shape[0]
    chunk = heads // pieces
    decay = jnp.broadcast_to(decay_total[:, None, None], (heads, 1, local_state.shape[2]))
    return pl.pallas_call(
        functools.partial(_chain_kernel, chunk),
        out_shape=jax.ShapeDtypeStruct(local_state.shape, local_state.dtype),
        in_specs=[pl.BlockSpec(memory_space=pltpu.VMEM)] * 2,
        out_specs=pl.BlockSpec(memory_space=pltpu.VMEM),
        scratch_shapes=[
            pltpu.VMEM(local_state.shape, local_state.dtype),
            pltpu.SemaphoreType.DMA((pieces,)),
            pltpu.SemaphoreType.DMA((pieces,)),
        ],
        compiler_params=pltpu.CompilerParams(collective_id=2, has_side_effects=True),
    )(local_state, decay)


group_heads = 8
highest = lax.Precision.HIGHEST


def from_behind(block, axis, distance):
    devices = range(lax.axis_size(axis))
    route = [(i - distance, i) for i in devices if i - distance in devices]
    return lax.ppermute(block, axis, route)


def local_terms(x_vals, b_vals, c_vals, dt_vals, cumulative, points, offset):
    row_count = x_vals.shape[0]
    x_wide = x_vals.astype(jnp.float32).reshape(row_count, H, P_SIZE)
    b_wide = b_vals.astype(jnp.float32)
    c_wide = c_vals.astype(jnp.float32)
    scores = lax.dot_general(
        c_vals, b_vals, (((1,), (1,)), ((), ())), preferred_element_type=jnp.float32
    )
    positions = jnp.arange(row_count, dtype=jnp.int32)
    causal = positions[:, None] >= positions[None, :]
    cum_heads = cumulative.T
    dt_heads = dt_vals.T

    def group_step(group_index, buffer):
        head_start = group_index * group_heads
        cum_group = lax.dynamic_slice_in_dim(cum_heads, head_start, group_heads, 0)
        dt_group = lax.dynamic_slice_in_dim(dt_heads, head_start, group_heads, 0)
        x_group = lax.dynamic_slice_in_dim(x_wide, head_start, group_heads, 1)
        spread = jnp.where(causal[None], cum_group[:, :, None] - cum_group[:, None, :], -1e30)
        weight = jnp.exp(spread) * dt_group[:, None, :] * scores[None]
        partial_value = jnp.einsum("hts,shp->thp", weight, x_group, precision=highest)
        return lax.dynamic_update_slice_in_dim(buffer, partial_value, head_start, 1)

    diagonal_part = lax.fori_loop(
        0, H // group_heads, group_step, jnp.zeros((row_count, H, P_SIZE), jnp.float32)
    )
    final_log = cumulative[row_count - 1]
    to_end = jnp.exp(final_log[None, :] - cumulative) * dt_vals
    decay_total = jnp.exp(final_log)
    local_state = jnp.einsum(
        "sk,sn->kn",
        (to_end[:, :, None] * x_wide).reshape(row_count, H * P_SIZE),
        b_wide,
        precision=highest,
    ).reshape(H, P_SIZE, N)
    local_index = points - offset
    owned_flag = ((local_index >= 0) & (local_index < row_count)).astype(jnp.float32)
    one_hot = (positions[None, :] == local_index[:, None]).astype(jnp.float32)
    cum_at = jnp.dot(one_hot, cumulative, precision=highest)
    before = positions[None, :] <= local_index[:, None]
    spread = jnp.where(before[:, :, None], cum_at[:, None, :] - cumulative[None], -1e30)
    read_weight = jnp.sum(owned_flag[:, None, None] * jnp.exp(spread), axis=0) * dt_vals / R
    carry_weight = jnp.sum(owned_flag[:, None] * jnp.exp(cum_at), axis=0) / R
    return (
        diagonal_part, x_wide, b_wide, c_wide, local_state, decay_total, to_end, read_weight, carry_weight
    )


def finish_block(diagonal_part, x_wide, c_wide, cumulative, h_in, gate_rows, d_skip, norm_gain):
    row_count = x_wide.shape[0]
    incoming = jnp.einsum("tn,hpn->thp", c_wide, h_in, precision=highest)
    ssm_out = (
        diagonal_part + jnp.exp(cumulative)[:, :, None] * incoming + d_skip[None, :, None] * x_wide
    )
    gated_out = ssm_out.reshape(row_count, H * P_SIZE) * jax.nn.silu(gate_rows.astype(jnp.float32))
    inv_rms = lax.rsqrt(jnp.mean(gated_out * gated_out, axis=-1, keepdims=True) + 1e-05)
    return (gated_out * inv_rms * norm_gain).astype(jnp.bfloat16)


def on_device(
    xbc,
    gate_input,
    dt_raw,
    conv_weight,
    conv_bias,
    dt_bias,
    a_rate,
    d_skip,
    norm_gain,
    labels,
    readout,
):
    row_count = xbc.shape[1]
    seq_count = lax.axis_size("seq")
    me = lax.axis_index("seq")
    n_one = jnp.sum(lax.all_gather(labels, "dp", tiled=True).astype(jnp.float32))
    edge_rows = from_behind(xbc[:, row_count - (KW - 1) :, :], "seq", 1)
    padded = jnp.concatenate([edge_rows, xbc], axis=1)[0].astype(jnp.float32)
    conv_sum = conv_bias
    for tap_index in range(KW):
        conv_sum = conv_sum + conv_weight[tap_index] * padded[tap_index : tap_index + row_count]
    activated = jax.nn.silu(conv_sum).astype(jnp.bfloat16)
    dt_vals = jax.nn.softplus(dt_raw[0].astype(jnp.float32) + dt_bias)
    cumulative = jnp.cumsum(-a_rate * dt_vals, axis=0)
    offset = me * row_count
    (diagonal_part, x_wide, b_wide, c_wide, local_state, decay_total, to_end, read_weight,
     carry_weight) = local_terms(
        activated[:, : H * P_SIZE],
        activated[:, H * P_SIZE : H * P_SIZE + N],
        activated[:, H * P_SIZE + N :],
        dt_vals,
        cumulative,
        readout[0],
        offset,
    )
    scalars = lax.all_gather(jnp.stack([decay_total, carry_weight]), "seq")
    coef_rows = [jnp.zeros_like(decay_total)]
    for later in range(seq_count - 1, 0, -1):
        coef_rows.append(scalars[later, 1] + scalars[later, 0] * coef_rows[-1])
    coef_all = jnp.stack(coef_rows[::-1])
    coef = jnp.sum(jnp.where((jnp.arange(seq_count) == me)[:, None], coef_all, 0.0), axis=0)
    mean_weight = coef[None, :] * to_end + read_weight
    mean_local = jnp.einsum(
        "sk,sn->kn",
        (mean_weight[:, :, None] * x_wide).reshape(row_count, H * P_SIZE),
        b_wide,
        precision=highest,
    )
    batch_count = lax.axis_size("dp")
    class_value = labels[0].astype(jnp.float32)
    class_weight = class_value / n_one - (1.0 - class_value) / (batch_count - n_one)
    partial_value = class_weight * mean_local
    block_rows = partial_value.shape[0] // (batch_count * seq_count)
    blocks = to_halving_order(partial_value, batch_count, seq_count, block_rows)
    steering = reduce_scatter_blocks(blocks)[0]
    h_in = carry_chain(local_state, decay_total)
    layer_out = finish_block(
        diagonal_part, x_wide, c_wide, cumulative, h_in, gate_input[0], d_skip, norm_gain
    )
    return (layer_out[None], steering)


def solution(mesh):
    return jax.shard_map(
        on_device,
        mesh=mesh,
        in_specs=(
            P("dp", "seq", None),
            P("dp", "seq", None),
            P("dp", "seq", None),
            P(),
            P(),
            P(),
            P(),
            P(),
            P(),
            P("dp"),
            P("dp", None),
        ),
        out_specs=(P("dp", "seq", None), P(("dp", "seq"), None)),
        check_vma=False,
    )
```

```python
import jax
import jax.numpy as jnp
from jax import lax
from jax.sharding import PartitionSpec as P
from jax.experimental import pallas as pl
from jax.experimental.pallas import tpu as pltpu
import functools

H = 40
P_SIZE = 64
N = 128
KW = 4
R = 4


MESH_ID = pl.DeviceIdType.MESH


def _halving_plan(dp_count, seq_count):
    plan = []
    bit = 1
    while bit < seq_count:
        plan.append(("seq", bit))
        bit *= 2
    bit = 1
    while bit < dp_count:
        plan.append(("dp", bit))
        bit *= 2
    return plan


def _reduce_scatter_kernel(plan, in_ref, label_ref, out_ref, acc, label_buf, label_send, label_recv, *rest):
    rounds = len(plan)
    recv = rest[:rounds]
    send_sem, recv_sem = rest[rounds], rest[rounds + 1]
    coords = {"dp": lax.axis_index("dp"), "seq": lax.axis_index("seq")}

    def partner_of(axis, bit):
        me = coords[axis]
        return me + bit - 2 * bit * ((me // bit) % 2)

    def device_of(axis, bit):
        if axis == "dp":
            return (partner_of(axis, bit), coords["seq"])
        return (coords["dp"], partner_of(axis, bit))

    dp_count = lax.axis_size("dp")

    def label_copy(shift):
        return pltpu.make_async_remote_copy(
            src_ref=label_ref,
            dst_ref=label_buf.at[shift],
            send_sem=label_send.at[shift],
            recv_sem=label_recv.at[shift],
            device_id=((coords["dp"] + shift) % dp_count, coords["seq"]),
            device_id_type=MESH_ID,
        )

    barrier = pltpu.get_barrier_semaphore()
    seq_rounds = [(axis, bit) for axis, bit in plan if axis == "seq"]
    for axis, bit in seq_rounds:
        pl.semaphore_signal(barrier, inc=1, device_id=device_of(axis, bit), device_id_type=MESH_ID)
    for shift in range(1, dp_count):
        pl.semaphore_signal(
            barrier, inc=1, device_id=((coords["dp"] + shift) % dp_count, coords["seq"]),
            device_id_type=MESH_ID,
        )
    pl.semaphore_wait(barrier, len(seq_rounds) + dp_count - 1)
    for shift in range(1, dp_count):
        label_copy(shift).start()

    size = in_ref.shape[0]
    base = 0
    copies = []
    for index, (axis, bit) in enumerate(plan):
        half = size // 2
        mine = (coords[axis] // bit) % 2
        keep = base + mine * half
        give = base + (1 - mine) * half
        if index == len(seq_rounds):
            for shift in range(1, dp_count):
                label_copy(shift).wait_recv()
            n_one = label_ref[...] + jnp.sum(label_buf[1:], axis=0)
            own = label_ref[...]
            weight = own / n_one - (1.0 - own) / (dp_count - n_one)
            acc[pl.ds(base, size)] = acc[pl.ds(base, size)] * weight[None]
        source = in_ref if index == 0 else acc
        copy = pltpu.make_async_remote_copy(
            src_ref=source.at[pl.ds(give, half)],
            dst_ref=recv[index],
            send_sem=send_sem.at[index],
            recv_sem=recv_sem.at[index],
            device_id=device_of(axis, bit),
            device_id_type=MESH_ID,
        )
        copy.start()
        copy.wait_recv()
        acc[pl.ds(keep, half)] = source[pl.ds(keep, half)] + recv[index][...]
        copies.append(copy)
        base = keep
        size = half
    out_ref[...] = acc[pl.ds(base, 1)]
    for copy in copies:
        copy.wait_send()
    for shift in range(1, dp_count):
        label_copy(shift).wait_send()


def reduce_scatter_blocks(blocks, label):
    dp_count = lax.axis_size("dp")
    seq_count = lax.axis_size("seq")
    plan = _halving_plan(dp_count, seq_count)
    n_blocks, rows, cols = blocks.shape
    recv_shapes = [pltpu.VMEM((n_blocks >> (i + 1), rows, cols), blocks.dtype) for i in range(len(plan))]
    return pl.pallas_call(
        functools.partial(_reduce_scatter_kernel, plan),
        out_shape=jax.ShapeDtypeStruct((1, rows, cols), blocks.dtype),
        in_specs=[pl.BlockSpec(memory_space=pltpu.VMEM)] * 2,
        out_specs=pl.BlockSpec(memory_space=pltpu.VMEM),
        scratch_shapes=[
            pltpu.VMEM((n_blocks, rows, cols), blocks.dtype),
            pltpu.VMEM((dp_count, 1, cols), jnp.float32),
            pltpu.SemaphoreType.DMA((dp_count,)),
            pltpu.SemaphoreType.DMA((dp_count,)),
        ] + recv_shapes + [
            pltpu.SemaphoreType.DMA((len(plan),)),
            pltpu.SemaphoreType.DMA((len(plan),)),
        ],
        compiler_params=pltpu.CompilerParams(collective_id=1, has_side_effects=True),
    )(blocks, jnp.broadcast_to(label.astype(jnp.float32), (1, cols)))


def to_halving_order(partial, dp_count, seq_count, rows):
    total_bits = (dp_count * seq_count).bit_length() - 1
    cols = partial.shape[-1]
    view = partial.reshape((2,) * total_bits + (rows, cols))
    order = tuple(range(total_bits - 1, -1, -1)) + (total_bits, total_bits + 1)
    return view.transpose(order).reshape(dp_count * seq_count, rows, cols)


def _chain_kernel(chunk, local_ref, decay_ref, hin_ref, send_buf, send_sem, recv_sem):
    count = lax.axis_size("seq")
    me = lax.axis_index("seq")
    row_id = lax.axis_index("dp")
    has_left = (me + count - 1) // count
    has_right = (2 * count - 2 - me) // count
    left = me - has_left
    right = me + has_right
    pieces = local_ref.shape[0] // chunk

    barrier = pltpu.get_barrier_semaphore()

    @pl.when(has_left == 1)
    def _():
        pl.semaphore_signal(barrier, inc=1, device_id=(row_id, left), device_id_type=MESH_ID)

    @pl.when(has_right == 1)
    def _():
        pl.semaphore_signal(barrier, inc=1, device_id=(row_id, right), device_id_type=MESH_ID)

    pl.semaphore_wait(barrier, has_left + has_right)

    def link(source, piece):
        rows = pl.ds(piece * chunk, chunk)
        return pltpu.make_async_remote_copy(
            src_ref=source.at[rows],
            dst_ref=hin_ref.at[rows],
            send_sem=send_sem.at[piece],
            recv_sem=recv_sem.at[piece],
            device_id=(row_id, right),
            device_id_type=MESH_ID,
        )

    @pl.when(has_left == 0)
    def _():
        hin_ref[...] = jnp.zeros_like(hin_ref)
        for piece in range(pieces):
            link(local_ref, piece).start()

    @pl.when(has_left == 1)
    def _():
        for piece in range(pieces):
            rows = pl.ds(piece * chunk, chunk)
            link(send_buf, piece).wait_recv()

            @pl.when(has_right == 1)
            def _():
                send_buf[rows] = decay_ref[rows] * hin_ref[rows] + local_ref[rows]
                link(send_buf, piece).start()

    @pl.when(has_right == 1)
    def _():
        for piece in range(pieces):
            link(send_buf, piece).wait_send()


def carry_chain(local_state, decay_total, pieces=8):
    heads = local_state.shape[0]
    chunk = heads // pieces
    decay = jnp.broadcast_to(decay_total[:, None, None], (heads, 1, local_state.shape[2]))
    return pl.pallas_call(
        functools.partial(_chain_kernel, chunk),
        out_shape=jax.ShapeDtypeStruct(local_state.shape, local_state.dtype),
        in_specs=[pl.BlockSpec(memory_space=pltpu.VMEM)] * 2,
        out_specs=pl.BlockSpec(memory_space=pltpu.VMEM),
        scratch_shapes=[
            pltpu.VMEM(local_state.shape, local_state.dtype),
            pltpu.SemaphoreType.DMA((pieces,)),
            pltpu.SemaphoreType.DMA((pieces,)),
        ],
        compiler_params=pltpu.CompilerParams(collective_id=2, has_side_effects=True),
    )(local_state, decay)


group_heads = 8
highest = lax.Precision.HIGHEST


def from_behind(block, axis, distance):
    devices = range(lax.axis_size(axis))
    route = [(i - distance, i) for i in devices if i - distance in devices]
    return lax.ppermute(block, axis, route)


def local_terms(x_vals, b_vals, c_vals, dt_vals, cumulative, points, offset):
    row_count = x_vals.shape[0]
    x_wide = x_vals.astype(jnp.float32).reshape(row_count, H, P_SIZE)
    b_wide = b_vals.astype(jnp.float32)
    c_wide = c_vals.astype(jnp.float32)
    scores = lax.dot_general(
        c_vals, b_vals, (((1,), (1,)), ((), ())), preferred_element_type=jnp.float32
    )
    positions = jnp.arange(row_count, dtype=jnp.int32)
    causal = positions[:, None] >= positions[None, :]
    cum_heads = cumulative.T
    dt_heads = dt_vals.T

    def group_step(group_index, buffer):
        head_start = group_index * group_heads
        cum_group = lax.dynamic_slice_in_dim(cum_heads, head_start, group_heads, 0)
        dt_group = lax.dynamic_slice_in_dim(dt_heads, head_start, group_heads, 0)
        x_group = lax.dynamic_slice_in_dim(x_wide, head_start, group_heads, 1)
        spread = jnp.where(causal[None], cum_group[:, :, None] - cum_group[:, None, :], -1e30)
        weight = jnp.exp(spread) * dt_group[:, None, :] * scores[None]
        partial_value = jnp.einsum("hts,shp->thp", weight, x_group, precision=highest)
        return lax.dynamic_update_slice_in_dim(buffer, partial_value, head_start, 1)

    diagonal_part = lax.fori_loop(
        0, H // group_heads, group_step, jnp.zeros((row_count, H, P_SIZE), jnp.float32)
    )
    final_log = cumulative[row_count - 1]
    to_end = jnp.exp(final_log[None, :] - cumulative) * dt_vals
    decay_total = jnp.exp(final_log)
    local_state = jnp.einsum(
        "sk,sn->kn",
        (to_end[:, :, None] * x_wide).reshape(row_count, H * P_SIZE),
        b_wide,
        precision=highest,
    ).reshape(H, P_SIZE, N)
    local_index = points - offset
    owned_flag = ((local_index >= 0) & (local_index < row_count)).astype(jnp.float32)
    one_hot = (positions[None, :] == local_index[:, None]).astype(jnp.float32)
    cum_at = jnp.dot(one_hot, cumulative, precision=highest)
    before = positions[None, :] <= local_index[:, None]
    spread = jnp.where(before[:, :, None], cum_at[:, None, :] - cumulative[None], -1e30)
    read_weight = jnp.sum(owned_flag[:, None, None] * jnp.exp(spread), axis=0) * dt_vals / R
    carry_weight = jnp.sum(owned_flag[:, None] * jnp.exp(cum_at), axis=0) / R
    return (
        diagonal_part, x_wide, b_wide, c_wide, local_state, decay_total, to_end, read_weight, carry_weight
    )


def finish_block(diagonal_part, x_wide, c_wide, cumulative, h_in, gate_rows, d_skip, norm_gain):
    row_count = x_wide.shape[0]
    incoming = jnp.einsum("tn,hpn->thp", c_wide, h_in, precision=highest)
    ssm_out = (
        diagonal_part + jnp.exp(cumulative)[:, :, None] * incoming + d_skip[None, :, None] * x_wide
    )
    gated_out = ssm_out.reshape(row_count, H * P_SIZE) * jax.nn.silu(gate_rows.astype(jnp.float32))
    inv_rms = lax.rsqrt(jnp.mean(gated_out * gated_out, axis=-1, keepdims=True) + 1e-05)
    return (gated_out * inv_rms * norm_gain).astype(jnp.bfloat16)


def on_device(
    xbc,
    gate_input,
    dt_raw,
    conv_weight,
    conv_bias,
    dt_bias,
    a_rate,
    d_skip,
    norm_gain,
    labels,
    readout,
):
    row_count = xbc.shape[1]
    seq_count = lax.axis_size("seq")
    me = lax.axis_index("seq")
    edge_rows = from_behind(xbc[:, row_count - (KW - 1) :, :], "seq", 1)
    padded = jnp.concatenate([edge_rows, xbc], axis=1)[0].astype(jnp.float32)
    conv_sum = conv_bias
    for tap_index in range(KW):
        conv_sum = conv_sum + conv_weight[tap_index] * padded[tap_index : tap_index + row_count]
    activated = jax.nn.silu(conv_sum).astype(jnp.bfloat16)
    dt_vals = jax.nn.softplus(dt_raw[0].astype(jnp.float32) + dt_bias)
    cumulative = jnp.cumsum(-a_rate * dt_vals, axis=0)
    offset = me * row_count
    (diagonal_part, x_wide, b_wide, c_wide, local_state, decay_total, to_end, read_weight,
     carry_weight) = local_terms(
        activated[:, : H * P_SIZE],
        activated[:, H * P_SIZE : H * P_SIZE + N],
        activated[:, H * P_SIZE + N :],
        dt_vals,
        cumulative,
        readout[0],
        offset,
    )
    h_in = carry_chain(local_state, decay_total)
    read_local = jnp.einsum(
        "sk,sn->kn",
        (read_weight[:, :, None] * x_wide).reshape(row_count, H * P_SIZE),
        b_wide,
        precision=highest,
    ).reshape(H, P_SIZE, N)
    mean_state = (carry_weight[:, None, None] * h_in + read_local).reshape(H * P_SIZE, N)
    batch_count = lax.axis_size("dp")
    block_rows = mean_state.shape[0] // (batch_count * seq_count)
    blocks = to_halving_order(mean_state, batch_count, seq_count, block_rows)
    steering = reduce_scatter_blocks(blocks, labels[0])[0]
    layer_out = finish_block(
        diagonal_part, x_wide, c_wide, cumulative, h_in, gate_input[0], d_skip, norm_gain
    )
    return (layer_out[None], steering)


def solution(mesh):
    return jax.shard_map(
        on_device,
        mesh=mesh,
        in_specs=(
            P("dp", "seq", None),
            P("dp", "seq", None),
            P("dp", "seq", None),
            P(),
            P(),
            P(),
            P(),
            P(),
            P(),
            P("dp"),
            P("dp", None),
        ),
        out_specs=(P("dp", "seq", None), P(("dp", "seq"), None)),
        check_vma=False,
    )
```

```python
import jax
import jax.numpy as jnp
from jax import lax
from jax.sharding import PartitionSpec as P
from jax.experimental import pallas as pl
from jax.experimental.pallas import tpu as pltpu
import functools

H = 40
P_SIZE = 64
N = 128
KW = 4
R = 4


MESH_ID = pl.DeviceIdType.MESH


def _halving_plan(dp_count, seq_count):
    plan = []
    bit = 1
    while bit < seq_count:
        plan.append(("seq", bit))
        bit *= 2
    bit = 1
    while bit < dp_count:
        plan.append(("dp", bit))
        bit *= 2
    return plan


def _reduce_scatter_kernel(plan, in_ref, label_ref, out_ref, acc, label_buf, label_send, label_recv, *rest):
    rounds = len(plan)
    recv = rest[:rounds]
    send_sem, recv_sem = rest[rounds], rest[rounds + 1]
    coords = {"dp": lax.axis_index("dp"), "seq": lax.axis_index("seq")}

    def partner_of(axis, bit):
        me = coords[axis]
        return me + bit - 2 * bit * ((me // bit) % 2)

    def device_of(axis, bit):
        if axis == "dp":
            return (partner_of(axis, bit), coords["seq"])
        return (coords["dp"], partner_of(axis, bit))

    dp_count = lax.axis_size("dp")

    def label_copy(shift):
        return pltpu.make_async_remote_copy(
            src_ref=label_ref,
            dst_ref=label_buf.at[shift],
            send_sem=label_send.at[shift],
            recv_sem=label_recv.at[shift],
            device_id=((coords["dp"] + shift) % dp_count, coords["seq"]),
            device_id_type=MESH_ID,
        )

    barrier = pltpu.get_barrier_semaphore()
    seq_rounds = [(axis, bit) for axis, bit in plan if axis == "seq"]
    for axis, bit in seq_rounds:
        pl.semaphore_signal(barrier, inc=1, device_id=device_of(axis, bit), device_id_type=MESH_ID)
    for shift in range(1, dp_count):
        pl.semaphore_signal(
            barrier, inc=1, device_id=((coords["dp"] + shift) % dp_count, coords["seq"]),
            device_id_type=MESH_ID,
        )
    pl.semaphore_wait(barrier, len(seq_rounds) + dp_count - 1)
    for shift in range(1, dp_count):
        label_copy(shift).start()

    size = in_ref.shape[0]
    base = 0
    copies = []
    for index, (axis, bit) in enumerate(plan):
        half = size // 2
        mine = (coords[axis] // bit) % 2
        keep = base + mine * half
        give = base + (1 - mine) * half
        if index == len(seq_rounds):
            for shift in range(1, dp_count):
                label_copy(shift).wait_recv()
            n_one = label_ref[...] + jnp.sum(label_buf[1:], axis=0)
            own = label_ref[...]
            weight = own / n_one - (1.0 - own) / (dp_count - n_one)
            acc[pl.ds(base, size)] = acc[pl.ds(base, size)] * weight[None]
        source = in_ref if index == 0 else acc
        copy = pltpu.make_async_remote_copy(
            src_ref=source.at[pl.ds(give, half)],
            dst_ref=recv[index],
            send_sem=send_sem.at[index],
            recv_sem=recv_sem.at[index],
            device_id=device_of(axis, bit),
            device_id_type=MESH_ID,
        )
        copy.start()
        copy.wait_recv()
        acc[pl.ds(keep, half)] = source[pl.ds(keep, half)] + recv[index][...]
        copies.append(copy)
        base = keep
        size = half
    out_ref[...] = acc[pl.ds(base, 1)]
    for copy in copies:
        copy.wait_send()
    for shift in range(1, dp_count):
        label_copy(shift).wait_send()


def reduce_scatter_blocks(blocks, label):
    dp_count = lax.axis_size("dp")
    seq_count = lax.axis_size("seq")
    plan = _halving_plan(dp_count, seq_count)
    n_blocks, rows, cols = blocks.shape
    recv_shapes = [pltpu.VMEM((n_blocks >> (i + 1), rows, cols), blocks.dtype) for i in range(len(plan))]
    return pl.pallas_call(
        functools.partial(_reduce_scatter_kernel, plan),
        out_shape=jax.ShapeDtypeStruct((1, rows, cols), blocks.dtype),
        in_specs=[pl.BlockSpec(memory_space=pltpu.VMEM)] * 2,
        out_specs=pl.BlockSpec(memory_space=pltpu.VMEM),
        scratch_shapes=[
            pltpu.VMEM((n_blocks, rows, cols), blocks.dtype),
            pltpu.VMEM((dp_count, 1, cols), jnp.float32),
            pltpu.SemaphoreType.DMA((dp_count,)),
            pltpu.SemaphoreType.DMA((dp_count,)),
        ] + recv_shapes + [
            pltpu.SemaphoreType.DMA((len(plan),)),
            pltpu.SemaphoreType.DMA((len(plan),)),
        ],
        compiler_params=pltpu.CompilerParams(collective_id=1, has_side_effects=True),
    )(blocks, jnp.broadcast_to(label.astype(jnp.float32), (1, cols)))


def to_halving_order(partial, dp_count, seq_count, rows):
    total_bits = (dp_count * seq_count).bit_length() - 1
    cols = partial.shape[-1]
    view = partial.reshape((2,) * total_bits + (rows, cols))
    order = tuple(range(total_bits - 1, -1, -1)) + (total_bits, total_bits + 1)
    return view.transpose(order).reshape(dp_count * seq_count, rows, cols)


def _chain_kernel(chunk, local_ref, decay_ref, hin_ref, send_buf, send_sem, recv_sem):
    count = lax.axis_size("seq")
    me = lax.axis_index("seq")
    row_id = lax.axis_index("dp")
    has_left = (me + count - 1) // count
    has_right = (2 * count - 2 - me) // count
    left = me - has_left
    right = me + has_right
    pieces = local_ref.shape[0] // chunk

    barrier = pltpu.get_barrier_semaphore()

    @pl.when(has_left == 1)
    def _():
        pl.semaphore_signal(barrier, inc=1, device_id=(row_id, left), device_id_type=MESH_ID)

    @pl.when(has_right == 1)
    def _():
        pl.semaphore_signal(barrier, inc=1, device_id=(row_id, right), device_id_type=MESH_ID)

    pl.semaphore_wait(barrier, has_left + has_right)

    def link(source, piece):
        rows = pl.ds(piece * chunk, chunk)
        return pltpu.make_async_remote_copy(
            src_ref=source.at[rows],
            dst_ref=hin_ref.at[rows],
            send_sem=send_sem.at[piece],
            recv_sem=recv_sem.at[piece],
            device_id=(row_id, right),
            device_id_type=MESH_ID,
        )

    @pl.when(has_left == 0)
    def _():
        hin_ref[...] = jnp.zeros_like(hin_ref)
        for piece in range(pieces):
            link(local_ref, piece).start()

    @pl.when(has_left == 1)
    def _():
        for piece in range(pieces):
            rows = pl.ds(piece * chunk, chunk)
            link(send_buf, piece).wait_recv()

            @pl.when(has_right == 1)
            def _():
                send_buf[rows] = decay_ref[rows] * hin_ref[rows] + local_ref[rows]
                link(send_buf, piece).start()

    @pl.when(has_right == 1)
    def _():
        for piece in range(pieces):
            link(send_buf, piece).wait_send()


def carry_chain(local_state, decay_total, pieces=20):
    heads = local_state.shape[0]
    chunk = heads // pieces
    decay = jnp.broadcast_to(decay_total[:, None, None], (heads, 1, local_state.shape[2]))
    return pl.pallas_call(
        functools.partial(_chain_kernel, chunk),
        out_shape=jax.ShapeDtypeStruct(local_state.shape, local_state.dtype),
        in_specs=[pl.BlockSpec(memory_space=pltpu.VMEM)] * 2,
        out_specs=pl.BlockSpec(memory_space=pltpu.VMEM),
        scratch_shapes=[
            pltpu.VMEM(local_state.shape, local_state.dtype),
            pltpu.SemaphoreType.DMA((pieces,)),
            pltpu.SemaphoreType.DMA((pieces,)),
        ],
        compiler_params=pltpu.CompilerParams(collective_id=2, has_side_effects=True),
    )(local_state, decay)


group_heads = 8
highest = lax.Precision.HIGHEST


def from_behind(block, axis, distance):
    devices = range(lax.axis_size(axis))
    route = [(i - distance, i) for i in devices if i - distance in devices]
    return lax.ppermute(block, axis, route)


def local_terms(x_vals, b_vals, c_vals, dt_vals, cumulative, points, offset):
    row_count = x_vals.shape[0]
    x_wide = x_vals.astype(jnp.float32).reshape(row_count, H, P_SIZE)
    b_wide = b_vals.astype(jnp.float32)
    c_wide = c_vals.astype(jnp.float32)
    scores = lax.dot_general(
        c_vals, b_vals, (((1,), (1,)), ((), ())), preferred_element_type=jnp.float32
    )
    positions = jnp.arange(row_count, dtype=jnp.int32)
    causal = positions[:, None] >= positions[None, :]
    cum_heads = cumulative.T
    dt_heads = dt_vals.T

    def group_step(group_index, buffer):
        head_start = group_index * group_heads
        cum_group = lax.dynamic_slice_in_dim(cum_heads, head_start, group_heads, 0)
        dt_group = lax.dynamic_slice_in_dim(dt_heads, head_start, group_heads, 0)
        x_group = lax.dynamic_slice_in_dim(x_wide, head_start, group_heads, 1)
        spread = jnp.where(causal[None], cum_group[:, :, None] - cum_group[:, None, :], -1e30)
        weight = jnp.exp(spread) * dt_group[:, None, :] * scores[None]
        partial_value = jnp.einsum("hts,shp->thp", weight, x_group, precision=highest)
        return lax.dynamic_update_slice_in_dim(buffer, partial_value, head_start, 1)

    diagonal_part = lax.fori_loop(
        0, H // group_heads, group_step, jnp.zeros((row_count, H, P_SIZE), jnp.float32)
    )
    final_log = cumulative[row_count - 1]
    to_end = jnp.exp(final_log[None, :] - cumulative) * dt_vals
    decay_total = jnp.exp(final_log)
    local_state = jnp.einsum(
        "sk,sn->kn",
        (to_end[:, :, None] * x_wide).reshape(row_count, H * P_SIZE),
        b_wide,
        precision=highest,
    ).reshape(H, P_SIZE, N)
    local_index = points - offset
    owned_flag = ((local_index >= 0) & (local_index < row_count)).astype(jnp.float32)
    one_hot = (positions[None, :] == local_index[:, None]).astype(jnp.float32)
    cum_at = jnp.dot(one_hot, cumulative, precision=highest)
    before = positions[None, :] <= local_index[:, None]
    spread = jnp.where(before[:, :, None], cum_at[:, None, :] - cumulative[None], -1e30)
    read_weight = jnp.sum(owned_flag[:, None, None] * jnp.exp(spread), axis=0) * dt_vals / R
    carry_weight = jnp.sum(owned_flag[:, None] * jnp.exp(cum_at), axis=0) / R
    return (
        diagonal_part, x_wide, b_wide, c_wide, local_state, decay_total, to_end, read_weight, carry_weight
    )


def finish_block(diagonal_part, x_wide, c_wide, cumulative, h_in, gate_rows, d_skip, norm_gain):
    row_count = x_wide.shape[0]
    incoming = jnp.einsum("tn,hpn->thp", c_wide, h_in, precision=highest)
    ssm_out = (
        diagonal_part + jnp.exp(cumulative)[:, :, None] * incoming + d_skip[None, :, None] * x_wide
    )
    gated_out = ssm_out.reshape(row_count, H * P_SIZE) * jax.nn.silu(gate_rows.astype(jnp.float32))
    inv_rms = lax.rsqrt(jnp.mean(gated_out * gated_out, axis=-1, keepdims=True) + 1e-05)
    return (gated_out * inv_rms * norm_gain).astype(jnp.bfloat16)


def on_device(
    xbc,
    gate_input,
    dt_raw,
    conv_weight,
    conv_bias,
    dt_bias,
    a_rate,
    d_skip,
    norm_gain,
    labels,
    readout,
):
    row_count = xbc.shape[1]
    seq_count = lax.axis_size("seq")
    me = lax.axis_index("seq")
    edge_rows = from_behind(xbc[:, row_count - (KW - 1) :, :], "seq", 1)
    padded = jnp.concatenate([edge_rows, xbc], axis=1)[0].astype(jnp.float32)
    conv_sum = conv_bias
    for tap_index in range(KW):
        conv_sum = conv_sum + conv_weight[tap_index] * padded[tap_index : tap_index + row_count]
    activated = jax.nn.silu(conv_sum).astype(jnp.bfloat16)
    dt_vals = jax.nn.softplus(dt_raw[0].astype(jnp.float32) + dt_bias)
    cumulative = jnp.cumsum(-a_rate * dt_vals, axis=0)
    offset = me * row_count
    (diagonal_part, x_wide, b_wide, c_wide, local_state, decay_total, to_end, read_weight,
     carry_weight) = local_terms(
        activated[:, : H * P_SIZE],
        activated[:, H * P_SIZE : H * P_SIZE + N],
        activated[:, H * P_SIZE + N :],
        dt_vals,
        cumulative,
        readout[0],
        offset,
    )
    h_in = carry_chain(local_state, decay_total)
    read_local = jnp.einsum(
        "sk,sn->kn",
        (read_weight[:, :, None] * x_wide).reshape(row_count, H * P_SIZE),
        b_wide,
        precision=highest,
    ).reshape(H, P_SIZE, N)
    mean_state = (carry_weight[:, None, None] * h_in + read_local).reshape(H * P_SIZE, N)
    batch_count = lax.axis_size("dp")
    block_rows = mean_state.shape[0] // (batch_count * seq_count)
    blocks = to_halving_order(mean_state, batch_count, seq_count, block_rows)
    steering = reduce_scatter_blocks(blocks, labels[0])[0]
    layer_out = finish_block(
        diagonal_part, x_wide, c_wide, cumulative, h_in, gate_input[0], d_skip, norm_gain
    )
    return (layer_out[None], steering)


def solution(mesh):
    return jax.shard_map(
        on_device,
        mesh=mesh,
        in_specs=(
            P("dp", "seq", None),
            P("dp", "seq", None),
            P("dp", "seq", None),
            P(),
            P(),
            P(),
            P(),
            P(),
            P(),
            P("dp"),
            P("dp", None),
        ),
        out_specs=(P("dp", "seq", None), P(("dp", "seq"), None)),
        check_vma=False,
    )
```

```python
import jax
import jax.numpy as jnp
from jax import lax
from jax.sharding import PartitionSpec as P
from jax.experimental import pallas as pl
from jax.experimental.pallas import tpu as pltpu
import functools

H = 40
P_SIZE = 64
N = 128
KW = 4
R = 4


MESH_ID = pl.DeviceIdType.MESH


def _halving_plan(dp_count, seq_count):
    plan = []
    bit = 1
    while bit < seq_count:
        plan.append(("seq", bit))
        bit *= 2
    bit = 1
    while bit < dp_count:
        plan.append(("dp", bit))
        bit *= 2
    return plan


def _reduce_scatter_kernel(plan, in_ref, label_ref, out_ref, acc, label_buf, label_send, label_recv, *rest):
    rounds = len(plan)
    recv = rest[:rounds]
    send_sem, recv_sem = rest[rounds], rest[rounds + 1]
    coords = {"dp": lax.axis_index("dp"), "seq": lax.axis_index("seq")}

    def partner_of(axis, bit):
        me = coords[axis]
        return me + bit - 2 * bit * ((me // bit) % 2)

    def device_of(axis, bit):
        if axis == "dp":
            return (partner_of(axis, bit), coords["seq"])
        return (coords["dp"], partner_of(axis, bit))

    dp_count = lax.axis_size("dp")

    def label_copy(shift):
        return pltpu.make_async_remote_copy(
            src_ref=label_ref,
            dst_ref=label_buf.at[shift],
            send_sem=label_send.at[shift],
            recv_sem=label_recv.at[shift],
            device_id=((coords["dp"] + shift) % dp_count, coords["seq"]),
            device_id_type=MESH_ID,
        )

    barrier = pltpu.get_barrier_semaphore()
    seq_rounds = [(axis, bit) for axis, bit in plan if axis == "seq"]
    for axis, bit in seq_rounds:
        pl.semaphore_signal(barrier, inc=1, device_id=device_of(axis, bit), device_id_type=MESH_ID)
    for shift in range(1, dp_count):
        pl.semaphore_signal(
            barrier, inc=1, device_id=((coords["dp"] + shift) % dp_count, coords["seq"]),
            device_id_type=MESH_ID,
        )
    pl.semaphore_wait(barrier, len(seq_rounds) + dp_count - 1)
    for shift in range(1, dp_count):
        label_copy(shift).start()

    size = in_ref.shape[0]
    base = 0
    copies = []
    for index, (axis, bit) in enumerate(plan):
        half = size // 2
        mine = (coords[axis] // bit) % 2
        keep = base + mine * half
        give = base + (1 - mine) * half
        if index == len(seq_rounds):
            for shift in range(1, dp_count):
                label_copy(shift).wait_recv()
            n_one = label_ref[...] + jnp.sum(label_buf[1:], axis=0)
            own = label_ref[...]
            weight = own / n_one - (1.0 - own) / (dp_count - n_one)
            acc[pl.ds(base, size)] = acc[pl.ds(base, size)] * weight[None]
        source = in_ref if index == 0 else acc
        copy = pltpu.make_async_remote_copy(
            src_ref=source.at[pl.ds(give, half)],
            dst_ref=recv[index],
            send_sem=send_sem.at[index],
            recv_sem=recv_sem.at[index],
            device_id=device_of(axis, bit),
            device_id_type=MESH_ID,
        )
        copy.start()
        copy.wait_recv()
        acc[pl.ds(keep, half)] = source[pl.ds(keep, half)] + recv[index][...]
        copies.append(copy)
        base = keep
        size = half
    out_ref[...] = acc[pl.ds(base, 1)]
    for copy in copies:
        copy.wait_send()
    for shift in range(1, dp_count):
        label_copy(shift).wait_send()


def reduce_scatter_blocks(blocks, label):
    dp_count = lax.axis_size("dp")
    seq_count = lax.axis_size("seq")
    plan = _halving_plan(dp_count, seq_count)
    n_blocks, rows, cols = blocks.shape
    recv_shapes = [pltpu.VMEM((n_blocks >> (i + 1), rows, cols), blocks.dtype) for i in range(len(plan))]
    return pl.pallas_call(
        functools.partial(_reduce_scatter_kernel, plan),
        out_shape=jax.ShapeDtypeStruct((1, rows, cols), blocks.dtype),
        in_specs=[pl.BlockSpec(memory_space=pltpu.VMEM)] * 2,
        out_specs=pl.BlockSpec(memory_space=pltpu.VMEM),
        scratch_shapes=[
            pltpu.VMEM((n_blocks, rows, cols), blocks.dtype),
            pltpu.VMEM((dp_count, 1, cols), jnp.float32),
            pltpu.SemaphoreType.DMA((dp_count,)),
            pltpu.SemaphoreType.DMA((dp_count,)),
        ] + recv_shapes + [
            pltpu.SemaphoreType.DMA((len(plan),)),
            pltpu.SemaphoreType.DMA((len(plan),)),
        ],
        compiler_params=pltpu.CompilerParams(collective_id=1, has_side_effects=True),
    )(blocks, jnp.broadcast_to(label.astype(jnp.float32), (1, cols)))


def to_halving_order(partial, dp_count, seq_count, rows):
    total_bits = (dp_count * seq_count).bit_length() - 1
    cols = partial.shape[-1]
    view = partial.reshape((2,) * total_bits + (rows, cols))
    order = tuple(range(total_bits - 1, -1, -1)) + (total_bits, total_bits + 1)
    return view.transpose(order).reshape(dp_count * seq_count, rows, cols)


def _chain_kernel(chunk, local_ref, decay_ref, hin_ref, send_buf, send_sem, recv_sem):
    count = lax.axis_size("seq")
    me = lax.axis_index("seq")
    row_id = lax.axis_index("dp")
    has_left = (me + count - 1) // count
    has_right = (2 * count - 2 - me) // count
    left = me - has_left
    right = me + has_right
    pieces = local_ref.shape[1] // chunk

    barrier = pltpu.get_barrier_semaphore()

    @pl.when(has_left == 1)
    def _():
        pl.semaphore_signal(barrier, inc=1, device_id=(row_id, left), device_id_type=MESH_ID)

    @pl.when(has_right == 1)
    def _():
        pl.semaphore_signal(barrier, inc=1, device_id=(row_id, right), device_id_type=MESH_ID)

    pl.semaphore_wait(barrier, has_left + has_right)

    def link(source, piece):
        cols = pl.ds(piece * chunk, chunk)
        return pltpu.make_async_remote_copy(
            src_ref=source.at[:, cols],
            dst_ref=hin_ref.at[:, cols],
            send_sem=send_sem.at[piece],
            recv_sem=recv_sem.at[piece],
            device_id=(row_id, right),
            device_id_type=MESH_ID,
        )

    @pl.when(has_left == 0)
    def _():
        hin_ref[...] = jnp.zeros_like(hin_ref)
        for piece in range(pieces):
            link(local_ref, piece).start()

    @pl.when(has_left == 1)
    def _():
        for piece in range(pieces):
            cols = pl.ds(piece * chunk, chunk)
            link(send_buf, piece).wait_recv()

            @pl.when(has_right == 1)
            def _():
                send_buf[:, cols] = decay_ref[:, cols] * hin_ref[:, cols] + local_ref[:, cols]
                link(send_buf, piece).start()

    @pl.when(has_right == 1)
    def _():
        for piece in range(pieces):
            link(send_buf, piece).wait_send()


def carry_chain(local_state, decay, pieces=20):
    chunk = local_state.shape[1] // pieces
    return pl.pallas_call(
        functools.partial(_chain_kernel, chunk),
        out_shape=jax.ShapeDtypeStruct(local_state.shape, local_state.dtype),
        in_specs=[pl.BlockSpec(memory_space=pltpu.VMEM)] * 2,
        out_specs=pl.BlockSpec(memory_space=pltpu.VMEM),
        scratch_shapes=[
            pltpu.VMEM(local_state.shape, local_state.dtype),
            pltpu.SemaphoreType.DMA((pieces,)),
            pltpu.SemaphoreType.DMA((pieces,)),
        ],
        compiler_params=pltpu.CompilerParams(collective_id=2, has_side_effects=True),
    )(local_state, decay)


group_heads = 8
highest = lax.Precision.HIGHEST


def from_behind(block, axis, distance):
    devices = range(lax.axis_size(axis))
    route = [(i - distance, i) for i in devices if i - distance in devices]
    return lax.ppermute(block, axis, route)


def state_product(weight, x_wide, b_wide):
    row_count = x_wide.shape[0]
    return lax.dot_general(
        b_wide,
        (weight[:, :, None] * x_wide).reshape(row_count, H * P_SIZE),
        (((0,), (0,)), ((), ())),
        precision=highest,
    )


def local_terms(x_vals, b_vals, c_vals, dt_vals, cumulative, points, offset):
    row_count = x_vals.shape[0]
    x_wide = x_vals.astype(jnp.float32).reshape(row_count, H, P_SIZE)
    b_wide = b_vals.astype(jnp.float32)
    c_wide = c_vals.astype(jnp.float32)
    scores = lax.dot_general(
        c_vals, b_vals, (((1,), (1,)), ((), ())), preferred_element_type=jnp.float32
    )
    positions = jnp.arange(row_count, dtype=jnp.int32)
    causal = positions[:, None] >= positions[None, :]
    cum_heads = cumulative.T
    dt_heads = dt_vals.T

    def group_step(group_index, buffer):
        head_start = group_index * group_heads
        cum_group = lax.dynamic_slice_in_dim(cum_heads, head_start, group_heads, 0)
        dt_group = lax.dynamic_slice_in_dim(dt_heads, head_start, group_heads, 0)
        x_group = lax.dynamic_slice_in_dim(x_wide, head_start, group_heads, 1)
        spread = jnp.where(causal[None], cum_group[:, :, None] - cum_group[:, None, :], -1e30)
        weight = jnp.exp(spread) * dt_group[:, None, :] * scores[None]
        partial_value = jnp.einsum("hts,shp->thp", weight, x_group, precision=highest)
        return lax.dynamic_update_slice_in_dim(buffer, partial_value, head_start, 1)

    diagonal_part = lax.fori_loop(
        0, H // group_heads, group_step, jnp.zeros((row_count, H, P_SIZE), jnp.float32)
    )
    final_log = cumulative[row_count - 1]
    to_end = jnp.exp(final_log[None, :] - cumulative) * dt_vals
    decay_total = jnp.exp(final_log)
    local_state = state_product(to_end, x_wide, b_wide)
    local_index = points - offset
    owned_flag = ((local_index >= 0) & (local_index < row_count)).astype(jnp.float32)
    one_hot = (positions[None, :] == local_index[:, None]).astype(jnp.float32)
    cum_at = jnp.dot(one_hot, cumulative, precision=highest)
    before = positions[None, :] <= local_index[:, None]
    spread = jnp.where(before[:, :, None], cum_at[:, None, :] - cumulative[None], -1e30)
    read_weight = jnp.sum(owned_flag[:, None, None] * jnp.exp(spread), axis=0) * dt_vals / R
    carry_weight = jnp.sum(owned_flag[:, None] * jnp.exp(cum_at), axis=0) / R
    return (
        diagonal_part, x_wide, b_wide, c_wide, local_state, decay_total, to_end, read_weight, carry_weight
    )


def finish_block(diagonal_part, x_wide, c_wide, cumulative, h_in, gate_rows, d_skip, norm_gain):
    row_count = x_wide.shape[0]
    incoming = jnp.dot(c_wide, h_in, precision=highest).reshape(row_count, H, P_SIZE)
    ssm_out = (
        diagonal_part + jnp.exp(cumulative)[:, :, None] * incoming + d_skip[None, :, None] * x_wide
    )
    gated_out = ssm_out.reshape(row_count, H * P_SIZE) * jax.nn.silu(gate_rows.astype(jnp.float32))
    inv_rms = lax.rsqrt(jnp.mean(gated_out * gated_out, axis=-1, keepdims=True) + 1e-05)
    return (gated_out * inv_rms * norm_gain).astype(jnp.bfloat16)


def on_device(
    xbc,
    gate_input,
    dt_raw,
    conv_weight,
    conv_bias,
    dt_bias,
    a_rate,
    d_skip,
    norm_gain,
    labels,
    readout,
):
    row_count = xbc.shape[1]
    seq_count = lax.axis_size("seq")
    me = lax.axis_index("seq")
    edge_rows = from_behind(xbc[:, row_count - (KW - 1) :, :], "seq", 1)
    padded = jnp.concatenate([edge_rows, xbc], axis=1)[0].astype(jnp.float32)
    conv_sum = conv_bias
    for tap_index in range(KW):
        conv_sum = conv_sum + conv_weight[tap_index] * padded[tap_index : tap_index + row_count]
    activated = jax.nn.silu(conv_sum).astype(jnp.bfloat16)
    dt_vals = jax.nn.softplus(dt_raw[0].astype(jnp.float32) + dt_bias)
    cumulative = jnp.cumsum(-a_rate * dt_vals, axis=0)
    offset = me * row_count
    (diagonal_part, x_wide, b_wide, c_wide, local_state, decay_total, to_end, read_weight,
     carry_weight) = local_terms(
        activated[:, : H * P_SIZE],
        activated[:, H * P_SIZE : H * P_SIZE + N],
        activated[:, H * P_SIZE + N :],
        dt_vals,
        cumulative,
        readout[0],
        offset,
    )
    h_in = carry_chain(local_state, jnp.repeat(decay_total, P_SIZE)[None])
    read_local = state_product(read_weight, x_wide, b_wide)
    mean_state = (jnp.repeat(carry_weight, P_SIZE)[None] * h_in + read_local).T
    batch_count = lax.axis_size("dp")
    block_rows = mean_state.shape[0] // (batch_count * seq_count)
    blocks = to_halving_order(mean_state, batch_count, seq_count, block_rows)
    steering = reduce_scatter_blocks(blocks, labels[0])[0]
    layer_out = finish_block(
        diagonal_part, x_wide, c_wide, cumulative, h_in, gate_input[0], d_skip, norm_gain
    )
    return (layer_out[None], steering)


def solution(mesh):
    return jax.shard_map(
        on_device,
        mesh=mesh,
        in_specs=(
            P("dp", "seq", None),
            P("dp", "seq", None),
            P("dp", "seq", None),
            P(),
            P(),
            P(),
            P(),
            P(),
            P(),
            P("dp"),
            P("dp", None),
        ),
        out_specs=(P("dp", "seq", None), P(("dp", "seq"), None)),
        check_vma=False,
    )
```

```python
import jax
import jax.numpy as jnp
from jax import lax
from jax.sharding import PartitionSpec as P
from jax.experimental import pallas as pl
from jax.experimental.pallas import tpu as pltpu
import functools

H = 40
P_SIZE = 64
N = 128
KW = 4
R = 4


MESH_ID = pl.DeviceIdType.MESH


def _halving_plan(dp_count, seq_count):
    plan = []
    bit = 1
    while bit < seq_count:
        plan.append(("seq", bit))
        bit *= 2
    bit = 1
    while bit < dp_count:
        plan.append(("dp", bit))
        bit *= 2
    return plan


def _reduce_scatter_kernel(plan, in_ref, label_ref, out_ref, acc, label_buf, label_send, label_recv, *rest):
    rounds = len(plan)
    recv = rest[:rounds]
    send_sem, recv_sem = rest[rounds], rest[rounds + 1]
    coords = {"dp": lax.axis_index("dp"), "seq": lax.axis_index("seq")}

    def partner_of(axis, bit):
        me = coords[axis]
        return me + bit - 2 * bit * ((me // bit) % 2)

    def device_of(axis, bit):
        if axis == "dp":
            return (partner_of(axis, bit), coords["seq"])
        return (coords["dp"], partner_of(axis, bit))

    dp_count = lax.axis_size("dp")

    def label_copy(shift):
        return pltpu.make_async_remote_copy(
            src_ref=label_ref,
            dst_ref=label_buf.at[shift],
            send_sem=label_send.at[shift],
            recv_sem=label_recv.at[shift],
            device_id=((coords["dp"] + shift) % dp_count, coords["seq"]),
            device_id_type=MESH_ID,
        )

    barrier = pltpu.get_barrier_semaphore()
    seq_rounds = [(axis, bit) for axis, bit in plan if axis == "seq"]
    for axis, bit in seq_rounds:
        pl.semaphore_signal(barrier, inc=1, device_id=device_of(axis, bit), device_id_type=MESH_ID)
    for shift in range(1, dp_count):
        pl.semaphore_signal(
            barrier, inc=1, device_id=((coords["dp"] + shift) % dp_count, coords["seq"]),
            device_id_type=MESH_ID,
        )
    pl.semaphore_wait(barrier, len(seq_rounds) + dp_count - 1)
    for shift in range(1, dp_count):
        label_copy(shift).start()

    size = in_ref.shape[0]
    base = 0
    copies = []
    for index, (axis, bit) in enumerate(plan):
        half = size // 2
        mine = (coords[axis] // bit) % 2
        keep = base + mine * half
        give = base + (1 - mine) * half
        if index == len(seq_rounds):
            for shift in range(1, dp_count):
                label_copy(shift).wait_recv()
            n_one = label_ref[...] + jnp.sum(label_buf[1:], axis=0)
            own = label_ref[...]
            weight = own / n_one - (1.0 - own) / (dp_count - n_one)
            acc[pl.ds(base, size)] = acc[pl.ds(base, size)] * weight[None]
        source = in_ref if index == 0 else acc
        copy = pltpu.make_async_remote_copy(
            src_ref=source.at[pl.ds(give, half)],
            dst_ref=recv[index],
            send_sem=send_sem.at[index],
            recv_sem=recv_sem.at[index],
            device_id=device_of(axis, bit),
            device_id_type=MESH_ID,
        )
        copy.start()
        copy.wait_recv()
        acc[pl.ds(keep, half)] = source[pl.ds(keep, half)] + recv[index][...]
        copies.append(copy)
        base = keep
        size = half
    out_ref[...] = acc[pl.ds(base, 1)]
    for copy in copies:
        copy.wait_send()
    for shift in range(1, dp_count):
        label_copy(shift).wait_send()


def reduce_scatter_blocks(blocks, label):
    dp_count = lax.axis_size("dp")
    seq_count = lax.axis_size("seq")
    plan = _halving_plan(dp_count, seq_count)
    n_blocks, rows, cols = blocks.shape
    recv_shapes = [pltpu.VMEM((n_blocks >> (i + 1), rows, cols), blocks.dtype) for i in range(len(plan))]
    return pl.pallas_call(
        functools.partial(_reduce_scatter_kernel, plan),
        out_shape=jax.ShapeDtypeStruct((1, rows, cols), blocks.dtype),
        in_specs=[pl.BlockSpec(memory_space=pltpu.VMEM)] * 2,
        out_specs=pl.BlockSpec(memory_space=pltpu.VMEM),
        scratch_shapes=[
            pltpu.VMEM((n_blocks, rows, cols), blocks.dtype),
            pltpu.VMEM((dp_count, 1, cols), jnp.float32),
            pltpu.SemaphoreType.DMA((dp_count,)),
            pltpu.SemaphoreType.DMA((dp_count,)),
        ] + recv_shapes + [
            pltpu.SemaphoreType.DMA((len(plan),)),
            pltpu.SemaphoreType.DMA((len(plan),)),
        ],
        compiler_params=pltpu.CompilerParams(collective_id=1, has_side_effects=True),
    )(blocks, jnp.broadcast_to(label.astype(jnp.float32), (1, cols)))


def to_halving_order(partial, dp_count, seq_count, rows):
    total_bits = (dp_count * seq_count).bit_length() - 1
    cols = partial.shape[-1]
    view = partial.reshape((2,) * total_bits + (rows, cols))
    order = tuple(range(total_bits - 1, -1, -1)) + (total_bits, total_bits + 1)
    return view.transpose(order).reshape(dp_count * seq_count, rows, cols)


def _chain_kernel(chunk, local_ref, decay_ref, hin_ref, send_buf, send_sem, recv_sem):
    count = lax.axis_size("seq")
    me = lax.axis_index("seq")
    row_id = lax.axis_index("dp")
    has_left = (me + count - 1) // count
    has_right = (2 * count - 2 - me) // count
    left = me - has_left
    right = me + has_right
    pieces = local_ref.shape[1] // chunk

    barrier = pltpu.get_barrier_semaphore()

    @pl.when(has_left == 1)
    def _():
        pl.semaphore_signal(barrier, inc=1, device_id=(row_id, left), device_id_type=MESH_ID)

    @pl.when(has_right == 1)
    def _():
        pl.semaphore_signal(barrier, inc=1, device_id=(row_id, right), device_id_type=MESH_ID)

    pl.semaphore_wait(barrier, has_left + has_right)

    def link(source, piece):
        cols = pl.ds(piece * chunk, chunk)
        return pltpu.make_async_remote_copy(
            src_ref=source.at[:, cols],
            dst_ref=hin_ref.at[:, cols],
            send_sem=send_sem.at[piece],
            recv_sem=recv_sem.at[piece],
            device_id=(row_id, right),
            device_id_type=MESH_ID,
        )

    @pl.when(has_left == 0)
    def _():
        hin_ref[...] = jnp.zeros_like(hin_ref)
        for piece in range(pieces):
            link(local_ref, piece).start()

    @pl.when(has_left == 1)
    def _():
        for piece in range(pieces):
            cols = pl.ds(piece * chunk, chunk)
            link(send_buf, piece).wait_recv()

            @pl.when(has_right == 1)
            def _():
                send_buf[:, cols] = decay_ref[:, cols] * hin_ref[:, cols] + local_ref[:, cols]
                link(send_buf, piece).start()

    @pl.when(has_right == 1)
    def _():
        for piece in range(pieces):
            link(send_buf, piece).wait_send()


def carry_chain(local_state, decay, pieces=20):
    chunk = local_state.shape[1] // pieces
    return pl.pallas_call(
        functools.partial(_chain_kernel, chunk),
        out_shape=jax.ShapeDtypeStruct(local_state.shape, local_state.dtype),
        in_specs=[pl.BlockSpec(memory_space=pltpu.VMEM)] * 2,
        out_specs=pl.BlockSpec(memory_space=pltpu.VMEM),
        scratch_shapes=[
            pltpu.VMEM(local_state.shape, local_state.dtype),
            pltpu.SemaphoreType.DMA((pieces,)),
            pltpu.SemaphoreType.DMA((pieces,)),
        ],
        compiler_params=pltpu.CompilerParams(collective_id=2, has_side_effects=True),
    )(local_state, decay)


group_heads = 8
highest = lax.Precision.HIGHEST


def from_behind(block, axis, distance):
    devices = range(lax.axis_size(axis))
    route = [(i - distance, i) for i in devices if i - distance in devices]
    return lax.ppermute(block, axis, route)


def state_product(weight, x_wide, b_wide):
    row_count = x_wide.shape[0]
    return lax.dot_general(
        b_wide,
        (weight[:, :, None] * x_wide).reshape(row_count, H * P_SIZE),
        (((0,), (0,)), ((), ())),
        precision=highest,
    )


def local_terms(x_vals, b_vals, c_vals, dt_vals, cumulative, points, offset):
    row_count = x_vals.shape[0]
    x_wide = x_vals.astype(jnp.float32).reshape(row_count, H, P_SIZE)
    b_wide = b_vals.astype(jnp.float32)
    c_wide = c_vals.astype(jnp.float32)
    scores = lax.dot_general(
        c_vals, b_vals, (((1,), (1,)), ((), ())), preferred_element_type=jnp.float32
    )
    positions = jnp.arange(row_count, dtype=jnp.int32)
    causal = positions[:, None] >= positions[None, :]
    masked_scores = jnp.where(causal, scores, 0.0)
    grow = jnp.exp(-cumulative) * dt_vals
    shrink = jnp.exp(cumulative)
    scaled_x = (grow[:, :, None] * x_wide).reshape(row_count, H * P_SIZE)
    mixed = jnp.dot(masked_scores, scaled_x, precision=highest).reshape(row_count, H, P_SIZE)
    diagonal_part = shrink[:, :, None] * mixed
    final_log = cumulative[row_count - 1]
    to_end = jnp.exp(final_log[None, :] - cumulative) * dt_vals
    decay_total = jnp.exp(final_log)
    local_state = state_product(to_end, x_wide, b_wide)
    local_index = points - offset
    owned_flag = ((local_index >= 0) & (local_index < row_count)).astype(jnp.float32)
    one_hot = (positions[None, :] == local_index[:, None]).astype(jnp.float32)
    cum_at = jnp.dot(one_hot, cumulative, precision=highest)
    before = positions[None, :] <= local_index[:, None]
    spread = jnp.where(before[:, :, None], cum_at[:, None, :] - cumulative[None], -1e30)
    read_weight = jnp.sum(owned_flag[:, None, None] * jnp.exp(spread), axis=0) * dt_vals / R
    carry_weight = jnp.sum(owned_flag[:, None] * jnp.exp(cum_at), axis=0) / R
    return (
        diagonal_part, x_wide, b_wide, c_wide, local_state, decay_total, to_end, read_weight, carry_weight
    )


def finish_block(diagonal_part, x_wide, c_wide, cumulative, h_in, gate_rows, d_skip, norm_gain):
    row_count = x_wide.shape[0]
    incoming = jnp.dot(c_wide, h_in, precision=highest).reshape(row_count, H, P_SIZE)
    ssm_out = (
        diagonal_part + jnp.exp(cumulative)[:, :, None] * incoming + d_skip[None, :, None] * x_wide
    )
    gated_out = ssm_out.reshape(row_count, H * P_SIZE) * jax.nn.silu(gate_rows.astype(jnp.float32))
    inv_rms = lax.rsqrt(jnp.mean(gated_out * gated_out, axis=-1, keepdims=True) + 1e-05)
    return (gated_out * inv_rms * norm_gain).astype(jnp.bfloat16)


def on_device(
    xbc,
    gate_input,
    dt_raw,
    conv_weight,
    conv_bias,
    dt_bias,
    a_rate,
    d_skip,
    norm_gain,
    labels,
    readout,
):
    row_count = xbc.shape[1]
    seq_count = lax.axis_size("seq")
    me = lax.axis_index("seq")
    edge_rows = from_behind(xbc[:, row_count - (KW - 1) :, :], "seq", 1)
    padded = jnp.concatenate([edge_rows, xbc], axis=1)[0].astype(jnp.float32)
    conv_sum = conv_bias
    for tap_index in range(KW):
        conv_sum = conv_sum + conv_weight[tap_index] * padded[tap_index : tap_index + row_count]
    activated = jax.nn.silu(conv_sum).astype(jnp.bfloat16)
    dt_vals = jax.nn.softplus(dt_raw[0].astype(jnp.float32) + dt_bias)
    cumulative = jnp.cumsum(-a_rate * dt_vals, axis=0)
    offset = me * row_count
    (diagonal_part, x_wide, b_wide, c_wide, local_state, decay_total, to_end, read_weight,
     carry_weight) = local_terms(
        activated[:, : H * P_SIZE],
        activated[:, H * P_SIZE : H * P_SIZE + N],
        activated[:, H * P_SIZE + N :],
        dt_vals,
        cumulative,
        readout[0],
        offset,
    )
    h_in = carry_chain(local_state, jnp.repeat(decay_total, P_SIZE)[None])
    read_local = state_product(read_weight, x_wide, b_wide)
    mean_state = (jnp.repeat(carry_weight, P_SIZE)[None] * h_in + read_local).T
    batch_count = lax.axis_size("dp")
    block_rows = mean_state.shape[0] // (batch_count * seq_count)
    blocks = to_halving_order(mean_state, batch_count, seq_count, block_rows)
    steering = reduce_scatter_blocks(blocks, labels[0])[0]
    layer_out = finish_block(
        diagonal_part, x_wide, c_wide, cumulative, h_in, gate_input[0], d_skip, norm_gain
    )
    return (layer_out[None], steering)


def solution(mesh):
    return jax.shard_map(
        on_device,
        mesh=mesh,
        in_specs=(
            P("dp", "seq", None),
            P("dp", "seq", None),
            P("dp", "seq", None),
            P(),
            P(),
            P(),
            P(),
            P(),
            P(),
            P("dp"),
            P("dp", None),
        ),
        out_specs=(P("dp", "seq", None), P(("dp", "seq"), None)),
        check_vma=False,
    )
```

```python
import jax
import jax.numpy as jnp
from jax import lax
from jax.sharding import PartitionSpec as P
from jax.experimental import pallas as pl
from jax.experimental.pallas import tpu as pltpu
import functools

H = 40
P_SIZE = 64
N = 128
KW = 4
R = 4


MESH_ID = pl.DeviceIdType.MESH


def _halving_plan(dp_count, seq_count):
    plan = []
    bit = 1
    while bit < seq_count:
        plan.append(("seq", bit))
        bit *= 2
    bit = 1
    while bit < dp_count:
        plan.append(("dp", bit))
        bit *= 2
    return plan


def _reduce_scatter_kernel(plan, in_ref, label_ref, out_ref, acc, label_buf, label_send, label_recv, *rest):
    rounds = len(plan)
    recv = rest[:rounds]
    send_sem, recv_sem = rest[rounds], rest[rounds + 1]
    coords = {"dp": lax.axis_index("dp"), "seq": lax.axis_index("seq")}

    y_count = lax.axis_size("seq") // 2
    core = coords["seq"] % 2
    y_virtual = (coords["seq"] // 2 + (y_count - 1) * core) % y_count

    def partner_of(axis, bit):
        me = coords[axis]
        if axis == "seq" and bit > 1:
            virtual = 2 * y_virtual + core
            other = virtual + bit - 2 * bit * ((virtual // bit) % 2)
            return 2 * ((other // 2 + y_count - (y_count - 1) * core) % y_count) + core
        return me + bit - 2 * bit * ((me // bit) % 2)

    def bit_of(axis, bit):
        if axis == "seq" and bit > 1:
            return ((2 * y_virtual + core) // bit) % 2
        return (coords[axis] // bit) % 2

    def device_of(axis, bit):
        if axis == "dp":
            return (partner_of(axis, bit), coords["seq"])
        return (coords["dp"], partner_of(axis, bit))

    dp_count = lax.axis_size("dp")

    def label_copy(shift):
        return pltpu.make_async_remote_copy(
            src_ref=label_ref,
            dst_ref=label_buf.at[shift],
            send_sem=label_send.at[shift],
            recv_sem=label_recv.at[shift],
            device_id=((coords["dp"] + shift) % dp_count, coords["seq"]),
            device_id_type=MESH_ID,
        )

    barrier = pltpu.get_barrier_semaphore()
    seq_rounds = [(axis, bit) for axis, bit in plan if axis == "seq"]
    for axis, bit in seq_rounds:
        pl.semaphore_signal(barrier, inc=1, device_id=device_of(axis, bit), device_id_type=MESH_ID)
    for shift in range(1, dp_count):
        pl.semaphore_signal(
            barrier, inc=1, device_id=((coords["dp"] + shift) % dp_count, coords["seq"]),
            device_id_type=MESH_ID,
        )
    pl.semaphore_wait(barrier, len(seq_rounds) + dp_count - 1)
    for shift in range(1, dp_count):
        label_copy(shift).start()

    size = in_ref.shape[0]
    base = 0
    copies = []
    for index, (axis, bit) in enumerate(plan):
        half = size // 2
        mine = bit_of(axis, bit)
        keep = base + mine * half
        give = base + (1 - mine) * half
        if index == len(seq_rounds):
            for shift in range(1, dp_count):
                label_copy(shift).wait_recv()
            n_one = label_ref[...] + jnp.sum(label_buf[1:], axis=0)
            own = label_ref[...]
            weight = own / n_one - (1.0 - own) / (dp_count - n_one)
            acc[pl.ds(base, size)] = acc[pl.ds(base, size)] * weight[None]
        source = in_ref if index == 0 else acc
        copy = pltpu.make_async_remote_copy(
            src_ref=source.at[pl.ds(give, half)],
            dst_ref=recv[index],
            send_sem=send_sem.at[index],
            recv_sem=recv_sem.at[index],
            device_id=device_of(axis, bit),
            device_id_type=MESH_ID,
        )
        copy.start()
        copy.wait_recv()
        acc[pl.ds(keep, half)] = source[pl.ds(keep, half)] + recv[index][...]
        copies.append(copy)
        base = keep
        size = half
    out_ref[...] = acc[pl.ds(base, 1)]
    for copy in copies:
        copy.wait_send()
    for shift in range(1, dp_count):
        label_copy(shift).wait_send()


def reduce_scatter_blocks(blocks, label):
    dp_count = lax.axis_size("dp")
    seq_count = lax.axis_size("seq")
    plan = _halving_plan(dp_count, seq_count)
    n_blocks, rows, cols = blocks.shape
    recv_shapes = [pltpu.VMEM((n_blocks >> (i + 1), rows, cols), blocks.dtype) for i in range(len(plan))]
    return pl.pallas_call(
        functools.partial(_reduce_scatter_kernel, plan),
        out_shape=jax.ShapeDtypeStruct((1, rows, cols), blocks.dtype),
        in_specs=[pl.BlockSpec(memory_space=pltpu.VMEM)] * 2,
        out_specs=pl.BlockSpec(memory_space=pltpu.VMEM),
        scratch_shapes=[
            pltpu.VMEM((n_blocks, rows, cols), blocks.dtype),
            pltpu.VMEM((dp_count, 1, cols), jnp.float32),
            pltpu.SemaphoreType.DMA((dp_count,)),
            pltpu.SemaphoreType.DMA((dp_count,)),
        ] + recv_shapes + [
            pltpu.SemaphoreType.DMA((len(plan),)),
            pltpu.SemaphoreType.DMA((len(plan),)),
        ],
        compiler_params=pltpu.CompilerParams(collective_id=1, has_side_effects=True),
    )(blocks, jnp.broadcast_to(label.astype(jnp.float32), (1, cols)))


def to_halving_order(partial, dp_count, seq_count, rows):
    total_bits = (dp_count * seq_count).bit_length() - 1
    cols = partial.shape[-1]
    view = partial.reshape((2,) * total_bits + (rows, cols))
    order = tuple(range(total_bits - 1, -1, -1)) + (total_bits, total_bits + 1)
    return view.transpose(order).reshape(dp_count * seq_count, rows, cols)


def _chain_kernel(chunk, local_ref, decay_ref, hin_ref, send_buf, send_sem, recv_sem):
    count = lax.axis_size("seq")
    me = lax.axis_index("seq")
    row_id = lax.axis_index("dp")
    has_left = (me + count - 1) // count
    has_right = (2 * count - 2 - me) // count
    left = me - has_left
    right = me + has_right
    pieces = local_ref.shape[1] // chunk

    barrier = pltpu.get_barrier_semaphore()

    @pl.when(has_left == 1)
    def _():
        pl.semaphore_signal(barrier, inc=1, device_id=(row_id, left), device_id_type=MESH_ID)

    @pl.when(has_right == 1)
    def _():
        pl.semaphore_signal(barrier, inc=1, device_id=(row_id, right), device_id_type=MESH_ID)

    pl.semaphore_wait(barrier, has_left + has_right)

    def link(source, piece):
        cols = pl.ds(piece * chunk, chunk)
        return pltpu.make_async_remote_copy(
            src_ref=source.at[:, cols],
            dst_ref=hin_ref.at[:, cols],
            send_sem=send_sem.at[piece],
            recv_sem=recv_sem.at[piece],
            device_id=(row_id, right),
            device_id_type=MESH_ID,
        )

    @pl.when(has_left == 0)
    def _():
        hin_ref[...] = jnp.zeros_like(hin_ref)
        for piece in range(pieces):
            link(local_ref, piece).start()

    @pl.when(has_left == 1)
    def _():
        for piece in range(pieces):
            cols = pl.ds(piece * chunk, chunk)
            link(send_buf, piece).wait_recv()

            @pl.when(has_right == 1)
            def _():
                send_buf[:, cols] = decay_ref[:, cols] * hin_ref[:, cols] + local_ref[:, cols]
                link(send_buf, piece).start()

    @pl.when(has_right == 1)
    def _():
        for piece in range(pieces):
            link(send_buf, piece).wait_send()


def carry_chain(local_state, decay, pieces=20):
    chunk = local_state.shape[1] // pieces
    return pl.pallas_call(
        functools.partial(_chain_kernel, chunk),
        out_shape=jax.ShapeDtypeStruct(local_state.shape, local_state.dtype),
        in_specs=[pl.BlockSpec(memory_space=pltpu.VMEM)] * 2,
        out_specs=pl.BlockSpec(memory_space=pltpu.VMEM),
        scratch_shapes=[
            pltpu.VMEM(local_state.shape, local_state.dtype),
            pltpu.SemaphoreType.DMA((pieces,)),
            pltpu.SemaphoreType.DMA((pieces,)),
        ],
        compiler_params=pltpu.CompilerParams(collective_id=2, has_side_effects=True),
    )(local_state, decay)


group_heads = 8
highest = lax.Precision.HIGHEST


def from_behind(block, axis, distance):
    devices = range(lax.axis_size(axis))
    route = [(i - distance, i) for i in devices if i - distance in devices]
    return lax.ppermute(block, axis, route)


def state_product(weight, x_wide, b_wide):
    row_count = x_wide.shape[0]
    return lax.dot_general(
        b_wide,
        (weight[:, :, None] * x_wide).reshape(row_count, H * P_SIZE),
        (((0,), (0,)), ((), ())),
        precision=highest,
    )


def local_terms(x_vals, b_vals, c_vals, dt_vals, cumulative, points, offset):
    row_count = x_vals.shape[0]
    x_wide = x_vals.astype(jnp.float32).reshape(row_count, H, P_SIZE)
    b_wide = b_vals.astype(jnp.float32)
    c_wide = c_vals.astype(jnp.float32)
    scores = lax.dot_general(
        c_vals, b_vals, (((1,), (1,)), ((), ())), preferred_element_type=jnp.float32
    )
    positions = jnp.arange(row_count, dtype=jnp.int32)
    causal = positions[:, None] >= positions[None, :]
    masked_scores = jnp.where(causal, scores, 0.0)
    grow = jnp.exp(-cumulative) * dt_vals
    shrink = jnp.exp(cumulative)
    scaled_x = (grow[:, :, None] * x_wide).reshape(row_count, H * P_SIZE)
    mixed = jnp.dot(masked_scores, scaled_x, precision=highest).reshape(row_count, H, P_SIZE)
    diagonal_part = shrink[:, :, None] * mixed
    final_log = cumulative[row_count - 1]
    to_end = jnp.exp(final_log[None, :] - cumulative) * dt_vals
    decay_total = jnp.exp(final_log)
    local_state = state_product(to_end, x_wide, b_wide)
    local_index = points - offset
    owned_flag = ((local_index >= 0) & (local_index < row_count)).astype(jnp.float32)
    one_hot = (positions[None, :] == local_index[:, None]).astype(jnp.float32)
    cum_at = jnp.dot(one_hot, cumulative, precision=highest)
    before = positions[None, :] <= local_index[:, None]
    spread = jnp.where(before[:, :, None], cum_at[:, None, :] - cumulative[None], -1e30)
    read_weight = jnp.sum(owned_flag[:, None, None] * jnp.exp(spread), axis=0) * dt_vals / R
    carry_weight = jnp.sum(owned_flag[:, None] * jnp.exp(cum_at), axis=0) / R
    return (
        diagonal_part, x_wide, b_wide, c_wide, local_state, decay_total, to_end, read_weight, carry_weight
    )


def finish_block(diagonal_part, x_wide, c_wide, cumulative, h_in, gate_rows, d_skip, norm_gain):
    row_count = x_wide.shape[0]
    incoming = jnp.dot(c_wide, h_in, precision=highest).reshape(row_count, H, P_SIZE)
    ssm_out = (
        diagonal_part + jnp.exp(cumulative)[:, :, None] * incoming + d_skip[None, :, None] * x_wide
    )
    gated_out = ssm_out.reshape(row_count, H * P_SIZE) * jax.nn.silu(gate_rows.astype(jnp.float32))
    inv_rms = lax.rsqrt(jnp.mean(gated_out * gated_out, axis=-1, keepdims=True) + 1e-05)
    return (gated_out * inv_rms * norm_gain).astype(jnp.bfloat16)


def on_device(
    xbc,
    gate_input,
    dt_raw,
    conv_weight,
    conv_bias,
    dt_bias,
    a_rate,
    d_skip,
    norm_gain,
    labels,
    readout,
):
    row_count = xbc.shape[1]
    seq_count = lax.axis_size("seq")
    me = lax.axis_index("seq")
    edge_rows = from_behind(xbc[:, row_count - (KW - 1) :, :], "seq", 1)
    padded = jnp.concatenate([edge_rows, xbc], axis=1)[0].astype(jnp.float32)
    conv_sum = conv_bias
    for tap_index in range(KW):
        conv_sum = conv_sum + conv_weight[tap_index] * padded[tap_index : tap_index + row_count]
    activated = jax.nn.silu(conv_sum).astype(jnp.bfloat16)
    dt_vals = jax.nn.softplus(dt_raw[0].astype(jnp.float32) + dt_bias)
    cumulative = jnp.cumsum(-a_rate * dt_vals, axis=0)
    offset = me * row_count
    (diagonal_part, x_wide, b_wide, c_wide, local_state, decay_total, to_end, read_weight,
     carry_weight) = local_terms(
        activated[:, : H * P_SIZE],
        activated[:, H * P_SIZE : H * P_SIZE + N],
        activated[:, H * P_SIZE + N :],
        dt_vals,
        cumulative,
        readout[0],
        offset,
    )
    h_in = carry_chain(local_state, jnp.repeat(decay_total, P_SIZE)[None])
    read_local = state_product(read_weight, x_wide, b_wide)
    mean_state = (jnp.repeat(carry_weight, P_SIZE)[None] * h_in + read_local).T
    batch_count = lax.axis_size("dp")
    block_rows = mean_state.shape[0] // (batch_count * seq_count)
    by_chip = mean_state.reshape(batch_count, seq_count // 2, 2, block_rows, N)
    by_chip = jnp.stack([by_chip[:, :, 0], jnp.roll(by_chip[:, :, 1], -1, axis=1)], axis=2)
    blocks = to_halving_order(by_chip.reshape(-1, N), batch_count, seq_count, block_rows)
    steering = reduce_scatter_blocks(blocks, labels[0])[0]
    layer_out = finish_block(
        diagonal_part, x_wide, c_wide, cumulative, h_in, gate_input[0], d_skip, norm_gain
    )
    return (layer_out[None], steering)


def solution(mesh):
    return jax.shard_map(
        on_device,
        mesh=mesh,
        in_specs=(
            P("dp", "seq", None),
            P("dp", "seq", None),
            P("dp", "seq", None),
            P(),
            P(),
            P(),
            P(),
            P(),
            P(),
            P("dp"),
            P("dp", None),
        ),
        out_specs=(P("dp", "seq", None), P(("dp", "seq"), None)),
        check_vma=False,
    )
```

```python
import jax
import jax.numpy as jnp
from jax import lax
from jax.sharding import PartitionSpec as P
from jax.experimental import pallas as pl
from jax.experimental.pallas import tpu as pltpu
import functools

H = 40
P_SIZE = 64
N = 128
KW = 4
R = 4


MESH_ID = pl.DeviceIdType.MESH


def _halving_plan(dp_count, seq_count):
    plan = []
    bit = 1
    while bit < seq_count:
        plan.append(("seq", bit))
        bit *= 2
    bit = 1
    while bit < dp_count:
        plan.append(("dp", bit))
        bit *= 2
    return plan


def _reduce_scatter_kernel(plan, in_ref, label_ref, out_ref, acc, label_buf, label_send, label_recv, *rest):
    rounds = len(plan)
    recv = rest[:rounds]
    send_sem, recv_sem = rest[rounds], rest[rounds + 1]
    coords = {"dp": lax.axis_index("dp"), "seq": lax.axis_index("seq")}

    def partner_of(axis, bit):
        me = coords[axis]
        return me + bit - 2 * bit * ((me // bit) % 2)

    def device_of(axis, bit):
        if axis == "dp":
            return (partner_of(axis, bit), coords["seq"])
        return (coords["dp"], partner_of(axis, bit))

    dp_count = lax.axis_size("dp")

    def label_copy(shift):
        return pltpu.make_async_remote_copy(
            src_ref=label_ref,
            dst_ref=label_buf.at[shift],
            send_sem=label_send.at[shift],
            recv_sem=label_recv.at[shift],
            device_id=((coords["dp"] + shift) % dp_count, coords["seq"]),
            device_id_type=MESH_ID,
        )

    barrier = pltpu.get_barrier_semaphore()
    seq_rounds = [(axis, bit) for axis, bit in plan if axis == "seq"]
    for axis, bit in seq_rounds:
        pl.semaphore_signal(barrier, inc=1, device_id=device_of(axis, bit), device_id_type=MESH_ID)
    for shift in range(1, dp_count):
        pl.semaphore_signal(
            barrier, inc=1, device_id=((coords["dp"] + shift) % dp_count, coords["seq"]),
            device_id_type=MESH_ID,
        )
    pl.semaphore_wait(barrier, len(seq_rounds) + dp_count - 1)
    for shift in range(1, dp_count):
        label_copy(shift).start()

    size = in_ref.shape[0]
    base = 0
    copies = []
    for index, (axis, bit) in enumerate(plan):
        half = size // 2
        mine = (coords[axis] // bit) % 2
        keep = base + mine * half
        give = base + (1 - mine) * half
        if index == len(seq_rounds):
            for shift in range(1, dp_count):
                label_copy(shift).wait_recv()
            n_one = label_ref[...] + jnp.sum(label_buf[1:], axis=0)
            own = label_ref[...]
            weight = own / n_one - (1.0 - own) / (dp_count - n_one)
            acc[pl.ds(base, size)] = acc[pl.ds(base, size)] * weight[None]
        source = in_ref if index == 0 else acc
        copy = pltpu.make_async_remote_copy(
            src_ref=source.at[pl.ds(give, half)],
            dst_ref=recv[index],
            send_sem=send_sem.at[index],
            recv_sem=recv_sem.at[index],
            device_id=device_of(axis, bit),
            device_id_type=MESH_ID,
        )
        copy.start()
        copy.wait_recv()
        acc[pl.ds(keep, half)] = source[pl.ds(keep, half)] + recv[index][...]
        copies.append(copy)
        base = keep
        size = half
    out_ref[...] = acc[pl.ds(base, 1)]
    for copy in copies:
        copy.wait_send()
    for shift in range(1, dp_count):
        label_copy(shift).wait_send()


def reduce_scatter_blocks(blocks, label):
    dp_count = lax.axis_size("dp")
    seq_count = lax.axis_size("seq")
    plan = _halving_plan(dp_count, seq_count)
    n_blocks, rows, cols = blocks.shape
    recv_shapes = [pltpu.VMEM((n_blocks >> (i + 1), rows, cols), blocks.dtype) for i in range(len(plan))]
    return pl.pallas_call(
        functools.partial(_reduce_scatter_kernel, plan),
        out_shape=jax.ShapeDtypeStruct((1, rows, cols), blocks.dtype),
        in_specs=[pl.BlockSpec(memory_space=pltpu.VMEM)] * 2,
        out_specs=pl.BlockSpec(memory_space=pltpu.VMEM),
        scratch_shapes=[
            pltpu.VMEM((n_blocks, rows, cols), blocks.dtype),
            pltpu.VMEM((dp_count, 1, cols), jnp.float32),
            pltpu.SemaphoreType.DMA((dp_count,)),
            pltpu.SemaphoreType.DMA((dp_count,)),
        ] + recv_shapes + [
            pltpu.SemaphoreType.DMA((len(plan),)),
            pltpu.SemaphoreType.DMA((len(plan),)),
        ],
        compiler_params=pltpu.CompilerParams(collective_id=1, has_side_effects=True),
    )(blocks, jnp.broadcast_to(label.astype(jnp.float32), (1, cols)))


def to_halving_order(partial, dp_count, seq_count, rows):
    total_bits = (dp_count * seq_count).bit_length() - 1
    cols = partial.shape[-1]
    view = partial.reshape((2,) * total_bits + (rows, cols))
    order = tuple(range(total_bits - 1, -1, -1)) + (total_bits, total_bits + 1)
    return view.transpose(order).reshape(dp_count * seq_count, rows, cols)


def _chain_kernel(chunk, local_ref, decay_ref, hin_ref, send_buf, send_sem, recv_sem):
    count = lax.axis_size("seq")
    me = lax.axis_index("seq")
    row_id = lax.axis_index("dp")
    has_left = (me + count - 1) // count
    has_right = (2 * count - 2 - me) // count
    left = me - has_left
    right = me + has_right
    pieces = local_ref.shape[1] // chunk

    barrier = pltpu.get_barrier_semaphore()

    @pl.when(has_left == 1)
    def _():
        pl.semaphore_signal(barrier, inc=1, device_id=(row_id, left), device_id_type=MESH_ID)

    @pl.when(has_right == 1)
    def _():
        pl.semaphore_signal(barrier, inc=1, device_id=(row_id, right), device_id_type=MESH_ID)

    pl.semaphore_wait(barrier, has_left + has_right)

    def link(source, piece):
        cols = pl.ds(piece * chunk, chunk)
        return pltpu.make_async_remote_copy(
            src_ref=source.at[:, cols],
            dst_ref=hin_ref.at[:, cols],
            send_sem=send_sem.at[piece],
            recv_sem=recv_sem.at[piece],
            device_id=(row_id, right),
            device_id_type=MESH_ID,
        )

    @pl.when(has_left == 0)
    def _():
        hin_ref[...] = jnp.zeros_like(hin_ref)
        for piece in range(pieces):
            link(local_ref, piece).start()

    @pl.when(has_left == 1)
    def _():
        for piece in range(pieces):
            cols = pl.ds(piece * chunk, chunk)
            link(send_buf, piece).wait_recv()

            @pl.when(has_right == 1)
            def _():
                send_buf[:, cols] = decay_ref[:, cols] * hin_ref[:, cols] + local_ref[:, cols]
                link(send_buf, piece).start()

    @pl.when(has_right == 1)
    def _():
        for piece in range(pieces):
            link(send_buf, piece).wait_send()


def carry_chain(local_state, decay, pieces=20):
    chunk = local_state.shape[1] // pieces
    return pl.pallas_call(
        functools.partial(_chain_kernel, chunk),
        out_shape=jax.ShapeDtypeStruct(local_state.shape, local_state.dtype),
        in_specs=[pl.BlockSpec(memory_space=pltpu.VMEM)] * 2,
        out_specs=pl.BlockSpec(memory_space=pltpu.VMEM),
        scratch_shapes=[
            pltpu.VMEM(local_state.shape, local_state.dtype),
            pltpu.SemaphoreType.DMA((pieces,)),
            pltpu.SemaphoreType.DMA((pieces,)),
        ],
        compiler_params=pltpu.CompilerParams(collective_id=2, has_side_effects=True),
    )(local_state, decay)


group_heads = 8
highest = lax.Precision.HIGHEST


def from_behind(block, axis, distance):
    devices = range(lax.axis_size(axis))
    route = [(i - distance, i) for i in devices if i - distance in devices]
    return lax.ppermute(block, axis, route)


def state_product(weight, x_wide, b_wide):
    row_count = x_wide.shape[0]
    return lax.dot_general(
        b_wide,
        (weight[:, :, None] * x_wide).reshape(row_count, H * P_SIZE),
        (((0,), (0,)), ((), ())),
        precision=highest,
    )


def local_terms(x_vals, b_vals, c_vals, dt_vals, cumulative, points, offset):
    row_count = x_vals.shape[0]
    x_wide = x_vals.astype(jnp.float32).reshape(row_count, H, P_SIZE)
    b_wide = b_vals.astype(jnp.float32)
    c_wide = c_vals.astype(jnp.float32)
    scores = lax.dot_general(
        c_vals, b_vals, (((1,), (1,)), ((), ())), preferred_element_type=jnp.float32
    )
    positions = jnp.arange(row_count, dtype=jnp.int32)
    causal = positions[:, None] >= positions[None, :]
    masked_scores = jnp.where(causal, scores, 0.0)
    grow = jnp.exp(-cumulative) * dt_vals
    shrink = jnp.exp(cumulative)
    scaled_x = (grow[:, :, None] * x_wide).reshape(row_count, H * P_SIZE)
    mixed = jnp.dot(masked_scores, scaled_x, precision=lax.Precision.HIGH).reshape(row_count, H, P_SIZE)
    diagonal_part = shrink[:, :, None] * mixed
    final_log = cumulative[row_count - 1]
    to_end = jnp.exp(final_log[None, :] - cumulative) * dt_vals
    decay_total = jnp.exp(final_log)
    local_state = state_product(to_end, x_wide, b_wide)
    local_index = points - offset
    owned_flag = ((local_index >= 0) & (local_index < row_count)).astype(jnp.float32)
    one_hot = (positions[None, :] == local_index[:, None]).astype(jnp.float32)
    cum_at = jnp.dot(one_hot, cumulative, precision=highest)
    before = positions[None, :] <= local_index[:, None]
    spread = jnp.where(before[:, :, None], cum_at[:, None, :] - cumulative[None], -1e30)
    read_weight = jnp.sum(owned_flag[:, None, None] * jnp.exp(spread), axis=0) * dt_vals / R
    carry_weight = jnp.sum(owned_flag[:, None] * jnp.exp(cum_at), axis=0) / R
    return (
        diagonal_part, x_wide, b_wide, c_wide, local_state, decay_total, to_end, read_weight, carry_weight
    )


def finish_block(diagonal_part, x_wide, c_wide, cumulative, h_in, gate_rows, d_skip, norm_gain):
    row_count = x_wide.shape[0]
    incoming = jnp.dot(c_wide, h_in, precision=lax.Precision.HIGH).reshape(row_count, H, P_SIZE)
    ssm_out = (
        diagonal_part + jnp.exp(cumulative)[:, :, None] * incoming + d_skip[None, :, None] * x_wide
    )
    gated_out = ssm_out.reshape(row_count, H * P_SIZE) * jax.nn.silu(gate_rows.astype(jnp.float32))
    inv_rms = lax.rsqrt(jnp.mean(gated_out * gated_out, axis=-1, keepdims=True) + 1e-05)
    return (gated_out * inv_rms * norm_gain).astype(jnp.bfloat16)


def on_device(
    xbc,
    gate_input,
    dt_raw,
    conv_weight,
    conv_bias,
    dt_bias,
    a_rate,
    d_skip,
    norm_gain,
    labels,
    readout,
):
    row_count = xbc.shape[1]
    seq_count = lax.axis_size("seq")
    me = lax.axis_index("seq")
    edge_rows = from_behind(xbc[:, row_count - (KW - 1) :, :], "seq", 1)
    padded = jnp.concatenate([edge_rows, xbc], axis=1)[0].astype(jnp.float32)
    conv_sum = conv_bias
    for tap_index in range(KW):
        conv_sum = conv_sum + conv_weight[tap_index] * padded[tap_index : tap_index + row_count]
    activated = jax.nn.silu(conv_sum).astype(jnp.bfloat16)
    dt_vals = jax.nn.softplus(dt_raw[0].astype(jnp.float32) + dt_bias)
    cumulative = jnp.cumsum(-a_rate * dt_vals, axis=0)
    offset = me * row_count
    (diagonal_part, x_wide, b_wide, c_wide, local_state, decay_total, to_end, read_weight,
     carry_weight) = local_terms(
        activated[:, : H * P_SIZE],
        activated[:, H * P_SIZE : H * P_SIZE + N],
        activated[:, H * P_SIZE + N :],
        dt_vals,
        cumulative,
        readout[0],
        offset,
    )
    h_in = carry_chain(local_state, jnp.repeat(decay_total, P_SIZE)[None])
    read_local = state_product(read_weight, x_wide, b_wide)
    mean_state = (jnp.repeat(carry_weight, P_SIZE)[None] * h_in + read_local).T
    batch_count = lax.axis_size("dp")
    block_rows = mean_state.shape[0] // (batch_count * seq_count)
    blocks = to_halving_order(mean_state, batch_count, seq_count, block_rows)
    steering = reduce_scatter_blocks(blocks, labels[0])[0]
    layer_out = finish_block(
        diagonal_part, x_wide, c_wide, cumulative, h_in, gate_input[0], d_skip, norm_gain
    )
    return (layer_out[None], steering)


def solution(mesh):
    return jax.shard_map(
        on_device,
        mesh=mesh,
        in_specs=(
            P("dp", "seq", None),
            P("dp", "seq", None),
            P("dp", "seq", None),
            P(),
            P(),
            P(),
            P(),
            P(),
            P(),
            P("dp"),
            P("dp", None),
        ),
        out_specs=(P("dp", "seq", None), P(("dp", "seq"), None)),
        check_vma=False,
    )
```

```python
import jax
import jax.numpy as jnp
from jax import lax
from jax.sharding import PartitionSpec as P
from jax.experimental import pallas as pl
from jax.experimental.pallas import tpu as pltpu
import functools

H = 40
P_SIZE = 64
N = 128
KW = 4
R = 4


MESH_ID = pl.DeviceIdType.MESH


def _halving_plan(dp_count, seq_count):
    plan = []
    bit = 1
    while bit < seq_count:
        plan.append(("seq", bit))
        bit *= 2
    bit = 1
    while bit < dp_count:
        plan.append(("dp", bit))
        bit *= 2
    return plan


def _reduce_scatter_kernel(plan, in_ref, label_ref, out_ref, acc, label_buf, label_send, label_recv, *rest):
    rounds = len(plan)
    recv = rest[:rounds]
    send_sem, recv_sem = rest[rounds], rest[rounds + 1]
    coords = {"dp": lax.axis_index("dp"), "seq": lax.axis_index("seq")}

    def partner_of(axis, bit):
        me = coords[axis]
        return me + bit - 2 * bit * ((me // bit) % 2)

    def device_of(axis, bit):
        if axis == "dp":
            return (partner_of(axis, bit), coords["seq"])
        return (coords["dp"], partner_of(axis, bit))

    dp_count = lax.axis_size("dp")

    def label_copy(shift):
        return pltpu.make_async_remote_copy(
            src_ref=label_ref,
            dst_ref=label_buf.at[shift],
            send_sem=label_send.at[shift],
            recv_sem=label_recv.at[shift],
            device_id=((coords["dp"] + shift) % dp_count, coords["seq"]),
            device_id_type=MESH_ID,
        )

    barrier = pltpu.get_barrier_semaphore()
    seq_rounds = [(axis, bit) for axis, bit in plan if axis == "seq"]
    for axis, bit in seq_rounds:
        pl.semaphore_signal(barrier, inc=1, device_id=device_of(axis, bit), device_id_type=MESH_ID)
    for shift in range(1, dp_count):
        pl.semaphore_signal(
            barrier, inc=1, device_id=((coords["dp"] + shift) % dp_count, coords["seq"]),
            device_id_type=MESH_ID,
        )
    pl.semaphore_wait(barrier, len(seq_rounds) + dp_count - 1)
    for shift in range(1, dp_count):
        label_copy(shift).start()

    size = in_ref.shape[0]
    base = 0
    copies = []
    for index, (axis, bit) in enumerate(plan):
        half = size // 2
        mine = (coords[axis] // bit) % 2
        keep = base + mine * half
        give = base + (1 - mine) * half
        if index == len(seq_rounds):
            for shift in range(1, dp_count):
                label_copy(shift).wait_recv()
            n_one = label_ref[...] + jnp.sum(label_buf[1:], axis=0)
            own = label_ref[...]
            weight = own / n_one - (1.0 - own) / (dp_count - n_one)
            acc[pl.ds(base, size)] = acc[pl.ds(base, size)] * weight[None]
        source = in_ref if index == 0 else acc
        copy = pltpu.make_async_remote_copy(
            src_ref=source.at[pl.ds(give, half)],
            dst_ref=recv[index],
            send_sem=send_sem.at[index],
            recv_sem=recv_sem.at[index],
            device_id=device_of(axis, bit),
            device_id_type=MESH_ID,
        )
        copy.start()
        copy.wait_recv()
        acc[pl.ds(keep, half)] = source[pl.ds(keep, half)] + recv[index][...]
        copies.append(copy)
        base = keep
        size = half
    out_ref[...] = acc[pl.ds(base, 1)]
    for copy in copies:
        copy.wait_send()
    for shift in range(1, dp_count):
        label_copy(shift).wait_send()


def reduce_scatter_blocks(blocks, label):
    dp_count = lax.axis_size("dp")
    seq_count = lax.axis_size("seq")
    plan = _halving_plan(dp_count, seq_count)
    n_blocks, rows, cols = blocks.shape
    recv_shapes = [pltpu.VMEM((n_blocks >> (i + 1), rows, cols), blocks.dtype) for i in range(len(plan))]
    return pl.pallas_call(
        functools.partial(_reduce_scatter_kernel, plan),
        out_shape=jax.ShapeDtypeStruct((1, rows, cols), blocks.dtype),
        in_specs=[pl.BlockSpec(memory_space=pltpu.VMEM)] * 2,
        out_specs=pl.BlockSpec(memory_space=pltpu.VMEM),
        scratch_shapes=[
            pltpu.VMEM((n_blocks, rows, cols), blocks.dtype),
            pltpu.VMEM((dp_count, 1, cols), jnp.float32),
            pltpu.SemaphoreType.DMA((dp_count,)),
            pltpu.SemaphoreType.DMA((dp_count,)),
        ] + recv_shapes + [
            pltpu.SemaphoreType.DMA((len(plan),)),
            pltpu.SemaphoreType.DMA((len(plan),)),
        ],
        compiler_params=pltpu.CompilerParams(collective_id=1, has_side_effects=True),
    )(blocks, jnp.broadcast_to(label.astype(jnp.float32), (1, cols)))


def to_halving_order(partial, dp_count, seq_count, rows):
    total_bits = (dp_count * seq_count).bit_length() - 1
    cols = partial.shape[-1]
    view = partial.reshape((2,) * total_bits + (rows, cols))
    order = tuple(range(total_bits - 1, -1, -1)) + (total_bits, total_bits + 1)
    return view.transpose(order).reshape(dp_count * seq_count, rows, cols)


def _chain_kernel(chunk, local_ref, decay_ref, hin_ref, send_buf, send_sem, recv_sem):
    count = lax.axis_size("seq")
    me = lax.axis_index("seq")
    row_id = lax.axis_index("dp")
    has_left = (me + count - 1) // count
    has_right = (2 * count - 2 - me) // count
    left = me - has_left
    right = me + has_right
    pieces = local_ref.shape[1] // chunk

    barrier = pltpu.get_barrier_semaphore()

    @pl.when(has_left == 1)
    def _():
        pl.semaphore_signal(barrier, inc=1, device_id=(row_id, left), device_id_type=MESH_ID)

    @pl.when(has_right == 1)
    def _():
        pl.semaphore_signal(barrier, inc=1, device_id=(row_id, right), device_id_type=MESH_ID)

    pl.semaphore_wait(barrier, has_left + has_right)

    def link(source, piece):
        cols = pl.ds(piece * chunk, chunk)
        return pltpu.make_async_remote_copy(
            src_ref=source.at[:, cols],
            dst_ref=hin_ref.at[:, cols],
            send_sem=send_sem.at[piece],
            recv_sem=recv_sem.at[piece],
            device_id=(row_id, right),
            device_id_type=MESH_ID,
        )

    @pl.when(has_left == 0)
    def _():
        hin_ref[...] = jnp.zeros_like(hin_ref)
        for piece in range(pieces):
            link(local_ref, piece).start()

    @pl.when(has_left == 1)
    def _():
        for piece in range(pieces):
            cols = pl.ds(piece * chunk, chunk)
            link(send_buf, piece).wait_recv()

            @pl.when(has_right == 1)
            def _():
                send_buf[:, cols] = decay_ref[:, cols] * hin_ref[:, cols] + local_ref[:, cols]
                link(send_buf, piece).start()

    @pl.when(has_right == 1)
    def _():
        for piece in range(pieces):
            link(send_buf, piece).wait_send()


def carry_chain(local_state, decay, pieces=20):
    chunk = local_state.shape[1] // pieces
    return pl.pallas_call(
        functools.partial(_chain_kernel, chunk),
        out_shape=jax.ShapeDtypeStruct(local_state.shape, local_state.dtype),
        in_specs=[pl.BlockSpec(memory_space=pltpu.VMEM)] * 2,
        out_specs=pl.BlockSpec(memory_space=pltpu.VMEM),
        scratch_shapes=[
            pltpu.VMEM(local_state.shape, local_state.dtype),
            pltpu.SemaphoreType.DMA((pieces,)),
            pltpu.SemaphoreType.DMA((pieces,)),
        ],
        compiler_params=pltpu.CompilerParams(collective_id=2, has_side_effects=True),
    )(local_state, decay)


group_heads = 8
highest = lax.Precision.HIGHEST


def from_behind(block, axis, distance):
    devices = range(lax.axis_size(axis))
    route = [(i - distance, i) for i in devices if i - distance in devices]
    return lax.ppermute(block, axis, route)


def state_product(weight, x_wide, b_wide):
    row_count = x_wide.shape[0]
    return lax.dot_general(
        b_wide,
        (weight[:, :, None] * x_wide).reshape(row_count, H * P_SIZE),
        (((0,), (0,)), ((), ())),
        precision=lax.Precision.HIGH,
    )


def local_terms(x_vals, b_vals, c_vals, dt_vals, cumulative, points, offset):
    row_count = x_vals.shape[0]
    x_wide = x_vals.astype(jnp.float32).reshape(row_count, H, P_SIZE)
    b_wide = b_vals.astype(jnp.float32)
    c_wide = c_vals.astype(jnp.float32)
    scores = lax.dot_general(
        c_vals, b_vals, (((1,), (1,)), ((), ())), preferred_element_type=jnp.float32
    )
    positions = jnp.arange(row_count, dtype=jnp.int32)
    causal = positions[:, None] >= positions[None, :]
    masked_scores = jnp.where(causal, scores, 0.0)
    grow = jnp.exp(-cumulative) * dt_vals
    shrink = jnp.exp(cumulative)
    scaled_x = (grow[:, :, None] * x_wide).reshape(row_count, H * P_SIZE)
    mixed = jnp.dot(masked_scores, scaled_x, precision=lax.Precision.HIGH).reshape(row_count, H, P_SIZE)
    diagonal_part = shrink[:, :, None] * mixed
    final_log = cumulative[row_count - 1]
    to_end = jnp.exp(final_log[None, :] - cumulative) * dt_vals
    decay_total = jnp.exp(final_log)
    local_state = state_product(to_end, x_wide, b_wide)
    local_index = points - offset
    owned_flag = ((local_index >= 0) & (local_index < row_count)).astype(jnp.float32)
    one_hot = (positions[None, :] == local_index[:, None]).astype(jnp.float32)
    cum_at = jnp.dot(one_hot, cumulative, precision=highest)
    before = positions[None, :] <= local_index[:, None]
    spread = jnp.where(before[:, :, None], cum_at[:, None, :] - cumulative[None], -1e30)
    read_weight = jnp.sum(owned_flag[:, None, None] * jnp.exp(spread), axis=0) * dt_vals / R
    carry_weight = jnp.sum(owned_flag[:, None] * jnp.exp(cum_at), axis=0) / R
    return (
        diagonal_part, x_wide, b_wide, c_wide, local_state, decay_total, to_end, read_weight, carry_weight
    )


def finish_block(diagonal_part, x_wide, c_wide, cumulative, h_in, gate_rows, d_skip, norm_gain):
    row_count = x_wide.shape[0]
    incoming = jnp.dot(c_wide, h_in, precision=lax.Precision.HIGH).reshape(row_count, H, P_SIZE)
    ssm_out = (
        diagonal_part + jnp.exp(cumulative)[:, :, None] * incoming + d_skip[None, :, None] * x_wide
    )
    gated_out = ssm_out.reshape(row_count, H * P_SIZE) * jax.nn.silu(gate_rows.astype(jnp.float32))
    inv_rms = lax.rsqrt(jnp.mean(gated_out * gated_out, axis=-1, keepdims=True) + 1e-05)
    return (gated_out * inv_rms * norm_gain).astype(jnp.bfloat16)


def on_device(
    xbc,
    gate_input,
    dt_raw,
    conv_weight,
    conv_bias,
    dt_bias,
    a_rate,
    d_skip,
    norm_gain,
    labels,
    readout,
):
    row_count = xbc.shape[1]
    seq_count = lax.axis_size("seq")
    me = lax.axis_index("seq")
    edge_rows = from_behind(xbc[:, row_count - (KW - 1) :, :], "seq", 1)
    padded = jnp.concatenate([edge_rows, xbc], axis=1)[0].astype(jnp.float32)
    conv_sum = conv_bias
    for tap_index in range(KW):
        conv_sum = conv_sum + conv_weight[tap_index] * padded[tap_index : tap_index + row_count]
    activated = jax.nn.silu(conv_sum).astype(jnp.bfloat16)
    dt_vals = jax.nn.softplus(dt_raw[0].astype(jnp.float32) + dt_bias)
    cumulative = jnp.cumsum(-a_rate * dt_vals, axis=0)
    offset = me * row_count
    (diagonal_part, x_wide, b_wide, c_wide, local_state, decay_total, to_end, read_weight,
     carry_weight) = local_terms(
        activated[:, : H * P_SIZE],
        activated[:, H * P_SIZE : H * P_SIZE + N],
        activated[:, H * P_SIZE + N :],
        dt_vals,
        cumulative,
        readout[0],
        offset,
    )
    h_in = carry_chain(local_state, jnp.repeat(decay_total, P_SIZE)[None])
    read_local = state_product(read_weight, x_wide, b_wide)
    mean_state = (jnp.repeat(carry_weight, P_SIZE)[None] * h_in + read_local).T
    batch_count = lax.axis_size("dp")
    block_rows = mean_state.shape[0] // (batch_count * seq_count)
    blocks = to_halving_order(mean_state, batch_count, seq_count, block_rows)
    steering = reduce_scatter_blocks(blocks, labels[0])[0]
    layer_out = finish_block(
        diagonal_part, x_wide, c_wide, cumulative, h_in, gate_input[0], d_skip, norm_gain
    )
    return (layer_out[None], steering)


def solution(mesh):
    return jax.shard_map(
        on_device,
        mesh=mesh,
        in_specs=(
            P("dp", "seq", None),
            P("dp", "seq", None),
            P("dp", "seq", None),
            P(),
            P(),
            P(),
            P(),
            P(),
            P(),
            P("dp"),
            P("dp", None),
        ),
        out_specs=(P("dp", "seq", None), P(("dp", "seq"), None)),
        check_vma=False,
    )
```

```python
import jax
import jax.numpy as jnp
from jax import lax
from jax.sharding import PartitionSpec as P
from jax.experimental import pallas as pl
from jax.experimental.pallas import tpu as pltpu
import functools

H = 40
P_SIZE = 64
N = 128
KW = 4
R = 4


MESH_ID = pl.DeviceIdType.MESH


def _halving_plan(dp_count, seq_count):
    plan = []
    bit = 1
    while bit < seq_count:
        plan.append(("seq", bit))
        bit *= 2
    bit = 1
    while bit < dp_count:
        plan.append(("dp", bit))
        bit *= 2
    return plan


def _reduce_scatter_kernel(plan, in_ref, label_ref, out_ref, acc, label_buf, label_send, label_recv, *rest):
    rounds = len(plan)
    recv = rest[:rounds]
    send_sem, recv_sem = rest[rounds], rest[rounds + 1]
    coords = {"dp": lax.axis_index("dp"), "seq": lax.axis_index("seq")}

    def partner_of(axis, bit):
        me = coords[axis]
        return me + bit - 2 * bit * ((me // bit) % 2)

    def device_of(axis, bit):
        if axis == "dp":
            return (partner_of(axis, bit), coords["seq"])
        return (coords["dp"], partner_of(axis, bit))

    dp_count = lax.axis_size("dp")

    def label_copy(shift):
        return pltpu.make_async_remote_copy(
            src_ref=label_ref,
            dst_ref=label_buf.at[shift],
            send_sem=label_send.at[shift],
            recv_sem=label_recv.at[shift],
            device_id=((coords["dp"] + shift) % dp_count, coords["seq"]),
            device_id_type=MESH_ID,
        )

    barrier = pltpu.get_barrier_semaphore()
    seq_rounds = [(axis, bit) for axis, bit in plan if axis == "seq"]
    for axis, bit in seq_rounds:
        pl.semaphore_signal(barrier, inc=1, device_id=device_of(axis, bit), device_id_type=MESH_ID)
    for shift in range(1, dp_count):
        pl.semaphore_signal(
            barrier, inc=1, device_id=((coords["dp"] + shift) % dp_count, coords["seq"]),
            device_id_type=MESH_ID,
        )
    pl.semaphore_wait(barrier, len(seq_rounds) + dp_count - 1)
    for shift in range(1, dp_count):
        label_copy(shift).start()

    size = in_ref.shape[0]
    base = 0
    copies = []
    for index, (axis, bit) in enumerate(plan):
        half = size // 2
        mine = (coords[axis] // bit) % 2
        keep = base + mine * half
        give = base + (1 - mine) * half
        if index == len(seq_rounds):
            for shift in range(1, dp_count):
                label_copy(shift).wait_recv()
            n_one = label_ref[...] + jnp.sum(label_buf[1:], axis=0)
            own = label_ref[...]
            weight = own / n_one - (1.0 - own) / (dp_count - n_one)
            acc[pl.ds(base, size)] = acc[pl.ds(base, size)] * weight[None]
        source = in_ref if index == 0 else acc
        copy = pltpu.make_async_remote_copy(
            src_ref=source.at[pl.ds(give, half)],
            dst_ref=recv[index],
            send_sem=send_sem.at[index],
            recv_sem=recv_sem.at[index],
            device_id=device_of(axis, bit),
            device_id_type=MESH_ID,
        )
        copy.start()
        copy.wait_recv()
        acc[pl.ds(keep, half)] = source[pl.ds(keep, half)] + recv[index][...]
        copies.append(copy)
        base = keep
        size = half
    out_ref[...] = acc[pl.ds(base, 1)]
    for copy in copies:
        copy.wait_send()
    for shift in range(1, dp_count):
        label_copy(shift).wait_send()


def reduce_scatter_blocks(blocks, label):
    dp_count = lax.axis_size("dp")
    seq_count = lax.axis_size("seq")
    plan = _halving_plan(dp_count, seq_count)
    n_blocks, rows, cols = blocks.shape
    recv_shapes = [pltpu.VMEM((n_blocks >> (i + 1), rows, cols), blocks.dtype) for i in range(len(plan))]
    return pl.pallas_call(
        functools.partial(_reduce_scatter_kernel, plan),
        out_shape=jax.ShapeDtypeStruct((1, rows, cols), blocks.dtype),
        in_specs=[pl.BlockSpec(memory_space=pltpu.VMEM)] * 2,
        out_specs=pl.BlockSpec(memory_space=pltpu.VMEM),
        scratch_shapes=[
            pltpu.VMEM((n_blocks, rows, cols), blocks.dtype),
            pltpu.VMEM((dp_count, 1, cols), jnp.float32),
            pltpu.SemaphoreType.DMA((dp_count,)),
            pltpu.SemaphoreType.DMA((dp_count,)),
        ] + recv_shapes + [
            pltpu.SemaphoreType.DMA((len(plan),)),
            pltpu.SemaphoreType.DMA((len(plan),)),
        ],
        compiler_params=pltpu.CompilerParams(collective_id=1, has_side_effects=True),
    )(blocks, jnp.broadcast_to(label.astype(jnp.float32), (1, cols)))


def to_halving_order(partial, dp_count, seq_count, rows):
    total_bits = (dp_count * seq_count).bit_length() - 1
    cols = partial.shape[-1]
    view = partial.reshape((2,) * total_bits + (rows, cols))
    order = tuple(range(total_bits - 1, -1, -1)) + (total_bits, total_bits + 1)
    return view.transpose(order).reshape(dp_count * seq_count, rows, cols)


def _chain_kernel(chunk, local_ref, decay_ref, hin_ref, send_buf, send_sem, recv_sem):
    count = lax.axis_size("seq")
    me = lax.axis_index("seq")
    row_id = lax.axis_index("dp")
    has_left = (me + count - 1) // count
    has_right = (2 * count - 2 - me) // count
    left = me - has_left
    right = me + has_right
    pieces = local_ref.shape[0] // chunk

    barrier = pltpu.get_barrier_semaphore()

    @pl.when(has_left == 1)
    def _():
        pl.semaphore_signal(barrier, inc=1, device_id=(row_id, left), device_id_type=MESH_ID)

    @pl.when(has_right == 1)
    def _():
        pl.semaphore_signal(barrier, inc=1, device_id=(row_id, right), device_id_type=MESH_ID)

    pl.semaphore_wait(barrier, has_left + has_right)

    def link(source, piece):
        cols = pl.ds(piece * chunk, chunk)
        return pltpu.make_async_remote_copy(
            src_ref=source.at[cols],
            dst_ref=hin_ref.at[cols],
            send_sem=send_sem.at[piece],
            recv_sem=recv_sem.at[piece],
            device_id=(row_id, right),
            device_id_type=MESH_ID,
        )

    @pl.when(has_left == 0)
    def _():
        hin_ref[...] = jnp.zeros_like(hin_ref)
        for piece in range(pieces):
            link(local_ref, piece).start()

    @pl.when(has_left == 1)
    def _():
        for piece in range(pieces):
            cols = pl.ds(piece * chunk, chunk)
            link(send_buf, piece).wait_recv()

            @pl.when(has_right == 1)
            def _():
                send_buf[cols] = decay_ref[...] * hin_ref[cols] + local_ref[cols]
                link(send_buf, piece).start()

    @pl.when(has_right == 1)
    def _():
        for piece in range(pieces):
            link(send_buf, piece).wait_send()


def carry_chain(local_state, decay, pieces=16):
    chunk = local_state.shape[0] // pieces
    return pl.pallas_call(
        functools.partial(_chain_kernel, chunk),
        out_shape=jax.ShapeDtypeStruct(local_state.shape, local_state.dtype),
        in_specs=[pl.BlockSpec(memory_space=pltpu.VMEM)] * 2,
        out_specs=pl.BlockSpec(memory_space=pltpu.VMEM),
        scratch_shapes=[
            pltpu.VMEM(local_state.shape, local_state.dtype),
            pltpu.SemaphoreType.DMA((pieces,)),
            pltpu.SemaphoreType.DMA((pieces,)),
        ],
        compiler_params=pltpu.CompilerParams(collective_id=2, has_side_effects=True),
    )(local_state, decay)


group_heads = 8
highest = lax.Precision.HIGHEST


def from_behind(block, axis, distance):
    devices = range(lax.axis_size(axis))
    route = [(i - distance, i) for i in devices if i - distance in devices]
    return lax.ppermute(block, axis, route)


def state_product(weight, x_wide, b_wide):
    row_count = x_wide.shape[0]
    return lax.dot_general(
        b_wide,
        (weight[:, :, None] * x_wide).reshape(row_count, H * P_SIZE),
        (((0,), (0,)), ((), ())),
        precision=lax.Precision.HIGH,
    )


def local_terms(x_vals, b_vals, c_vals, dt_vals, cumulative, points, offset):
    row_count = x_vals.shape[0]
    x_wide = x_vals.astype(jnp.float32).reshape(row_count, H, P_SIZE)
    b_wide = b_vals.astype(jnp.float32)
    c_wide = c_vals.astype(jnp.float32)
    scores = lax.dot_general(
        c_vals, b_vals, (((1,), (1,)), ((), ())), preferred_element_type=jnp.float32
    )
    positions = jnp.arange(row_count, dtype=jnp.int32)
    causal = positions[:, None] >= positions[None, :]
    masked_scores = jnp.where(causal, scores, 0.0)
    grow = jnp.exp(-cumulative) * dt_vals
    shrink = jnp.exp(cumulative)
    scaled_x = (grow[:, :, None] * x_wide).reshape(row_count, H * P_SIZE)
    mixed = jnp.dot(masked_scores, scaled_x, precision=lax.Precision.HIGH).reshape(row_count, H, P_SIZE)
    diagonal_part = shrink[:, :, None] * mixed
    final_log = cumulative[row_count - 1]
    to_end = jnp.exp(final_log[None, :] - cumulative) * dt_vals
    decay_total = jnp.exp(final_log)
    local_state = state_product(to_end, x_wide, b_wide)
    local_index = points - offset
    owned_flag = ((local_index >= 0) & (local_index < row_count)).astype(jnp.float32)
    one_hot = (positions[None, :] == local_index[:, None]).astype(jnp.float32)
    cum_at = jnp.dot(one_hot, cumulative, precision=highest)
    before = positions[None, :] <= local_index[:, None]
    spread = jnp.where(before[:, :, None], cum_at[:, None, :] - cumulative[None], -1e30)
    read_weight = jnp.sum(owned_flag[:, None, None] * jnp.exp(spread), axis=0) * dt_vals / R
    carry_weight = jnp.sum(owned_flag[:, None] * jnp.exp(cum_at), axis=0) / R
    return (
        diagonal_part, x_wide, b_wide, c_wide, local_state, decay_total, to_end, read_weight, carry_weight
    )


def finish_block(diagonal_part, x_wide, c_wide, cumulative, h_in, gate_rows, d_skip, norm_gain):
    row_count = x_wide.shape[0]
    incoming = jnp.dot(c_wide, h_in, precision=lax.Precision.HIGH).reshape(row_count, H, P_SIZE)
    ssm_out = (
        diagonal_part + jnp.exp(cumulative)[:, :, None] * incoming + d_skip[None, :, None] * x_wide
    )
    gated_out = ssm_out.reshape(row_count, H * P_SIZE) * jax.nn.silu(gate_rows.astype(jnp.float32))
    inv_rms = lax.rsqrt(jnp.mean(gated_out * gated_out, axis=-1, keepdims=True) + 1e-05)
    return (gated_out * inv_rms * norm_gain).astype(jnp.bfloat16)


def on_device(
    xbc,
    gate_input,
    dt_raw,
    conv_weight,
    conv_bias,
    dt_bias,
    a_rate,
    d_skip,
    norm_gain,
    labels,
    readout,
):
    row_count = xbc.shape[1]
    seq_count = lax.axis_size("seq")
    me = lax.axis_index("seq")
    edge_rows = from_behind(xbc[:, row_count - (KW - 1) :, :], "seq", 1)
    padded = jnp.concatenate([edge_rows, xbc], axis=1)[0].astype(jnp.float32)
    conv_sum = conv_bias
    for tap_index in range(KW):
        conv_sum = conv_sum + conv_weight[tap_index] * padded[tap_index : tap_index + row_count]
    activated = jax.nn.silu(conv_sum).astype(jnp.bfloat16)
    dt_vals = jax.nn.softplus(dt_raw[0].astype(jnp.float32) + dt_bias)
    cumulative = jnp.cumsum(-a_rate * dt_vals, axis=0)
    offset = me * row_count
    (diagonal_part, x_wide, b_wide, c_wide, local_state, decay_total, to_end, read_weight,
     carry_weight) = local_terms(
        activated[:, : H * P_SIZE],
        activated[:, H * P_SIZE : H * P_SIZE + N],
        activated[:, H * P_SIZE + N :],
        dt_vals,
        cumulative,
        readout[0],
        offset,
    )
    h_in = carry_chain(local_state, jnp.repeat(decay_total, P_SIZE)[None])
    read_local = state_product(read_weight, x_wide, b_wide)
    mean_state = (jnp.repeat(carry_weight, P_SIZE)[None] * h_in + read_local).T
    batch_count = lax.axis_size("dp")
    block_rows = mean_state.shape[0] // (batch_count * seq_count)
    blocks = to_halving_order(mean_state, batch_count, seq_count, block_rows)
    steering = reduce_scatter_blocks(blocks, labels[0])[0]
    layer_out = finish_block(
        diagonal_part, x_wide, c_wide, cumulative, h_in, gate_input[0], d_skip, norm_gain
    )
    return (layer_out[None], steering)


def solution(mesh):
    return jax.shard_map(
        on_device,
        mesh=mesh,
        in_specs=(
            P("dp", "seq", None),
            P("dp", "seq", None),
            P("dp", "seq", None),
            P(),
            P(),
            P(),
            P(),
            P(),
            P(),
            P("dp"),
            P("dp", None),
        ),
        out_specs=(P("dp", "seq", None), P(("dp", "seq"), None)),
        check_vma=False,
    )
```

```python
import jax
import jax.numpy as jnp
from jax import lax
from jax.sharding import PartitionSpec as P
from jax.experimental import pallas as pl
from jax.experimental.pallas import tpu as pltpu
import functools

H = 40
P_SIZE = 64
N = 128
KW = 4
R = 4


MESH_ID = pl.DeviceIdType.MESH


def _halving_plan(dp_count, seq_count):
    plan = []
    bit = 1
    while bit < seq_count:
        plan.append(("seq", bit))
        bit *= 2
    bit = 1
    while bit < dp_count:
        plan.append(("dp", bit))
        bit *= 2
    return plan


def _reduce_scatter_kernel(plan, in_ref, label_ref, out_ref, acc, label_buf, label_send, label_recv, *rest):
    rounds = len(plan)
    recv = rest[:rounds]
    send_sem, recv_sem = rest[rounds], rest[rounds + 1]
    coords = {"dp": lax.axis_index("dp"), "seq": lax.axis_index("seq")}

    def partner_of(axis, bit):
        me = coords[axis]
        return me + bit - 2 * bit * ((me // bit) % 2)

    def device_of(axis, bit):
        if axis == "dp":
            return (partner_of(axis, bit), coords["seq"])
        return (coords["dp"], partner_of(axis, bit))

    dp_count = lax.axis_size("dp")

    def label_copy(shift):
        return pltpu.make_async_remote_copy(
            src_ref=label_ref,
            dst_ref=label_buf.at[shift],
            send_sem=label_send.at[shift],
            recv_sem=label_recv.at[shift],
            device_id=((coords["dp"] + shift) % dp_count, coords["seq"]),
            device_id_type=MESH_ID,
        )

    barrier = pltpu.get_barrier_semaphore()
    seq_rounds = [(axis, bit) for axis, bit in plan if axis == "seq"]
    for axis, bit in seq_rounds:
        pl.semaphore_signal(barrier, inc=1, device_id=device_of(axis, bit), device_id_type=MESH_ID)
    for shift in range(1, dp_count):
        pl.semaphore_signal(
            barrier, inc=1, device_id=((coords["dp"] + shift) % dp_count, coords["seq"]),
            device_id_type=MESH_ID,
        )
    pl.semaphore_wait(barrier, len(seq_rounds) + dp_count - 1)
    for shift in range(1, dp_count):
        label_copy(shift).start()

    size = in_ref.shape[0]
    base = 0
    copies = []
    for index, (axis, bit) in enumerate(plan):
        half = size // 2
        mine = (coords[axis] // bit) % 2
        keep = base + mine * half
        give = base + (1 - mine) * half
        if index == len(seq_rounds):
            for shift in range(1, dp_count):
                label_copy(shift).wait_recv()
            n_one = label_ref[...] + jnp.sum(label_buf[1:], axis=0)
            own = label_ref[...]
            weight = own / n_one - (1.0 - own) / (dp_count - n_one)
            acc[pl.ds(base, size)] = acc[pl.ds(base, size)] * weight[None]
        source = in_ref if index == 0 else acc
        copy = pltpu.make_async_remote_copy(
            src_ref=source.at[pl.ds(give, half)],
            dst_ref=recv[index],
            send_sem=send_sem.at[index],
            recv_sem=recv_sem.at[index],
            device_id=device_of(axis, bit),
            device_id_type=MESH_ID,
        )
        copy.start()
        copy.wait_recv()
        acc[pl.ds(keep, half)] = source[pl.ds(keep, half)] + recv[index][...]
        copies.append(copy)
        base = keep
        size = half
    out_ref[...] = acc[pl.ds(base, 1)]
    for copy in copies:
        copy.wait_send()
    for shift in range(1, dp_count):
        label_copy(shift).wait_send()


def reduce_scatter_blocks(blocks, label):
    dp_count = lax.axis_size("dp")
    seq_count = lax.axis_size("seq")
    plan = _halving_plan(dp_count, seq_count)
    n_blocks, rows, cols = blocks.shape
    recv_shapes = [pltpu.VMEM((n_blocks >> (i + 1), rows, cols), blocks.dtype) for i in range(len(plan))]
    return pl.pallas_call(
        functools.partial(_reduce_scatter_kernel, plan),
        out_shape=jax.ShapeDtypeStruct((1, rows, cols), blocks.dtype),
        in_specs=[pl.BlockSpec(memory_space=pltpu.VMEM)] * 2,
        out_specs=pl.BlockSpec(memory_space=pltpu.VMEM),
        scratch_shapes=[
            pltpu.VMEM((n_blocks, rows, cols), blocks.dtype),
            pltpu.VMEM((dp_count, 1, cols), jnp.float32),
            pltpu.SemaphoreType.DMA((dp_count,)),
            pltpu.SemaphoreType.DMA((dp_count,)),
        ] + recv_shapes + [
            pltpu.SemaphoreType.DMA((len(plan),)),
            pltpu.SemaphoreType.DMA((len(plan),)),
        ],
        compiler_params=pltpu.CompilerParams(collective_id=1, has_side_effects=True),
    )(blocks, jnp.broadcast_to(label.astype(jnp.float32), (1, cols)))


def to_halving_order(partial, dp_count, seq_count, rows):
    total_bits = (dp_count * seq_count).bit_length() - 1
    cols = partial.shape[-1]
    view = partial.reshape((2,) * total_bits + (rows, cols))
    order = tuple(range(total_bits - 1, -1, -1)) + (total_bits, total_bits + 1)
    return view.transpose(order).reshape(dp_count * seq_count, rows, cols)


def _chain_kernel(chunk, local_ref, decay_ref, hin_ref, send_buf, send_sem, recv_sem):
    count = lax.axis_size("seq")
    me = lax.axis_index("seq")
    row_id = lax.axis_index("dp")
    has_left = (me + count - 1) // count
    has_right = (2 * count - 2 - me) // count
    left = me - has_left
    right = me + has_right
    pieces = local_ref.shape[1] // chunk

    barrier = pltpu.get_barrier_semaphore()

    @pl.when(has_left == 1)
    def _():
        pl.semaphore_signal(barrier, inc=1, device_id=(row_id, left), device_id_type=MESH_ID)

    @pl.when(has_right == 1)
    def _():
        pl.semaphore_signal(barrier, inc=1, device_id=(row_id, right), device_id_type=MESH_ID)

    pl.semaphore_wait(barrier, has_left + has_right)

    def link(source, piece):
        cols = pl.ds(piece * chunk, chunk)
        return pltpu.make_async_remote_copy(
            src_ref=source.at[:, cols],
            dst_ref=hin_ref.at[:, cols],
            send_sem=send_sem.at[piece],
            recv_sem=recv_sem.at[piece],
            device_id=(row_id, right),
            device_id_type=MESH_ID,
        )

    @pl.when(has_left == 0)
    def _():
        for piece in range(pieces):
            link(local_ref, piece).start()
        hin_ref[...] = jnp.zeros_like(hin_ref)

    @pl.when(has_left == 1)
    def _():
        for piece in range(pieces):
            cols = pl.ds(piece * chunk, chunk)
            link(send_buf, piece).wait_recv()

            @pl.when(has_right == 1)
            def _():
                send_buf[:, cols] = decay_ref[:, cols] * hin_ref[:, cols] + local_ref[:, cols]
                link(send_buf, piece).start()

    @pl.when(has_right == 1)
    def _():
        for piece in range(pieces):
            link(send_buf, piece).wait_send()


def carry_chain(local_state, decay, pieces=20):
    chunk = local_state.shape[1] // pieces
    return pl.pallas_call(
        functools.partial(_chain_kernel, chunk),
        out_shape=jax.ShapeDtypeStruct(local_state.shape, local_state.dtype),
        in_specs=[pl.BlockSpec(memory_space=pltpu.VMEM)] * 2,
        out_specs=pl.BlockSpec(memory_space=pltpu.VMEM),
        scratch_shapes=[
            pltpu.VMEM(local_state.shape, local_state.dtype),
            pltpu.SemaphoreType.DMA((pieces,)),
            pltpu.SemaphoreType.DMA((pieces,)),
        ],
        compiler_params=pltpu.CompilerParams(collective_id=2, has_side_effects=True),
    )(local_state, decay)


group_heads = 8
highest = lax.Precision.HIGHEST


def from_behind(block, axis, distance):
    devices = range(lax.axis_size(axis))
    route = [(i - distance, i) for i in devices if i - distance in devices]
    return lax.ppermute(block, axis, route)


def state_product(weight, x_wide, b_wide):
    row_count = x_wide.shape[0]
    return lax.dot_general(
        b_wide,
        (weight[:, :, None] * x_wide).reshape(row_count, H * P_SIZE),
        (((0,), (0,)), ((), ())),
        precision=lax.Precision.HIGH,
    )


def local_terms(x_vals, b_vals, c_vals, dt_vals, cumulative, points, offset):
    row_count = x_vals.shape[0]
    x_wide = x_vals.astype(jnp.float32).reshape(row_count, H, P_SIZE)
    b_wide = b_vals.astype(jnp.float32)
    c_wide = c_vals.astype(jnp.float32)
    scores = lax.dot_general(
        c_vals, b_vals, (((1,), (1,)), ((), ())), preferred_element_type=jnp.float32
    )
    positions = jnp.arange(row_count, dtype=jnp.int32)
    causal = positions[:, None] >= positions[None, :]
    masked_scores = jnp.where(causal, scores, 0.0)
    grow = jnp.exp(-cumulative) * dt_vals
    shrink = jnp.exp(cumulative)
    scaled_x = (grow[:, :, None] * x_wide).reshape(row_count, H * P_SIZE)
    mixed = jnp.dot(masked_scores, scaled_x, precision=lax.Precision.HIGH).reshape(row_count, H, P_SIZE)
    diagonal_part = shrink[:, :, None] * mixed
    final_log = cumulative[row_count - 1]
    to_end = jnp.exp(final_log[None, :] - cumulative) * dt_vals
    decay_total = jnp.exp(final_log)
    local_state = state_product(to_end, x_wide, b_wide)
    local_index = points - offset
    owned_flag = ((local_index >= 0) & (local_index < row_count)).astype(jnp.float32)
    one_hot = (positions[None, :] == local_index[:, None]).astype(jnp.float32)
    cum_at = jnp.dot(one_hot, cumulative, precision=highest)
    before = positions[None, :] <= local_index[:, None]
    spread = jnp.where(before[:, :, None], cum_at[:, None, :] - cumulative[None], -1e30)
    read_weight = jnp.sum(owned_flag[:, None, None] * jnp.exp(spread), axis=0) * dt_vals / R
    carry_weight = jnp.sum(owned_flag[:, None] * jnp.exp(cum_at), axis=0) / R
    return (
        diagonal_part, x_wide, b_wide, c_wide, local_state, decay_total, to_end, read_weight, carry_weight
    )


def finish_block(diagonal_part, x_wide, c_wide, cumulative, h_in, gate_rows, d_skip, norm_gain):
    row_count = x_wide.shape[0]
    incoming = jnp.dot(c_wide, h_in, precision=lax.Precision.HIGH).reshape(row_count, H, P_SIZE)
    ssm_out = (
        diagonal_part + jnp.exp(cumulative)[:, :, None] * incoming + d_skip[None, :, None] * x_wide
    )
    gated_out = ssm_out.reshape(row_count, H * P_SIZE) * jax.nn.silu(gate_rows.astype(jnp.float32))
    inv_rms = lax.rsqrt(jnp.mean(gated_out * gated_out, axis=-1, keepdims=True) + 1e-05)
    return (gated_out * inv_rms * norm_gain).astype(jnp.bfloat16)


def on_device(
    xbc,
    gate_input,
    dt_raw,
    conv_weight,
    conv_bias,
    dt_bias,
    a_rate,
    d_skip,
    norm_gain,
    labels,
    readout,
):
    row_count = xbc.shape[1]
    seq_count = lax.axis_size("seq")
    me = lax.axis_index("seq")
    edge_rows = from_behind(xbc[:, row_count - (KW - 1) :, :], "seq", 1)
    padded = jnp.concatenate([edge_rows, xbc], axis=1)[0].astype(jnp.float32)
    conv_sum = conv_bias
    for tap_index in range(KW):
        conv_sum = conv_sum + conv_weight[tap_index] * padded[tap_index : tap_index + row_count]
    activated = jax.nn.silu(conv_sum).astype(jnp.bfloat16)
    dt_vals = jax.nn.softplus(dt_raw[0].astype(jnp.float32) + dt_bias)
    cumulative = jnp.cumsum(-a_rate * dt_vals, axis=0)
    offset = me * row_count
    (diagonal_part, x_wide, b_wide, c_wide, local_state, decay_total, to_end, read_weight,
     carry_weight) = local_terms(
        activated[:, : H * P_SIZE],
        activated[:, H * P_SIZE : H * P_SIZE + N],
        activated[:, H * P_SIZE + N :],
        dt_vals,
        cumulative,
        readout[0],
        offset,
    )
    h_in = carry_chain(local_state, jnp.repeat(decay_total, P_SIZE)[None])
    read_local = state_product(read_weight, x_wide, b_wide)
    mean_state = (jnp.repeat(carry_weight, P_SIZE)[None] * h_in + read_local).T
    batch_count = lax.axis_size("dp")
    block_rows = mean_state.shape[0] // (batch_count * seq_count)
    blocks = to_halving_order(mean_state, batch_count, seq_count, block_rows)
    steering = reduce_scatter_blocks(blocks, labels[0])[0]
    layer_out = finish_block(
        diagonal_part, x_wide, c_wide, cumulative, h_in, gate_input[0], d_skip, norm_gain
    )
    return (layer_out[None], steering)


def solution(mesh):
    return jax.shard_map(
        on_device,
        mesh=mesh,
        in_specs=(
            P("dp", "seq", None),
            P("dp", "seq", None),
            P("dp", "seq", None),
            P(),
            P(),
            P(),
            P(),
            P(),
            P(),
            P("dp"),
            P("dp", None),
        ),
        out_specs=(P("dp", "seq", None), P(("dp", "seq"), None)),
        check_vma=False,
    )
```

```python
import jax
import jax.numpy as jnp
from jax import lax
from jax.sharding import PartitionSpec as P
from jax.experimental import pallas as pl
from jax.experimental.pallas import tpu as pltpu
import functools

H = 40
P_SIZE = 64
N = 128
KW = 4
R = 4


MESH_ID = pl.DeviceIdType.MESH


def _halving_plan(dp_count, seq_count):
    plan = []
    bit = 1
    while bit < seq_count:
        plan.append(("seq", bit))
        bit *= 2
    bit = 1
    while bit < dp_count:
        plan.append(("dp", bit))
        bit *= 2
    return plan


def _reduce_scatter_kernel(plan, in_ref, label_ref, out_ref, acc, label_buf, label_send, label_recv, *rest):
    rounds = len(plan)
    recv = rest[:rounds]
    send_sem, recv_sem = rest[rounds], rest[rounds + 1]
    coords = {"dp": lax.axis_index("dp"), "seq": lax.axis_index("seq")}

    def partner_of(axis, bit):
        me = coords[axis]
        return me + bit - 2 * bit * ((me // bit) % 2)

    def device_of(axis, bit):
        if axis == "dp":
            return (partner_of(axis, bit), coords["seq"])
        return (coords["dp"], partner_of(axis, bit))

    dp_count = lax.axis_size("dp")

    def label_copy(shift):
        return pltpu.make_async_remote_copy(
            src_ref=label_ref,
            dst_ref=label_buf.at[shift],
            send_sem=label_send.at[shift],
            recv_sem=label_recv.at[shift],
            device_id=((coords["dp"] + shift) % dp_count, coords["seq"]),
            device_id_type=MESH_ID,
        )

    barrier = pltpu.get_barrier_semaphore()
    seq_rounds = [(axis, bit) for axis, bit in plan if axis == "seq"]
    for axis, bit in seq_rounds:
        pl.semaphore_signal(barrier, inc=1, device_id=device_of(axis, bit), device_id_type=MESH_ID)
    for shift in range(1, dp_count):
        pl.semaphore_signal(
            barrier, inc=1, device_id=((coords["dp"] + shift) % dp_count, coords["seq"]),
            device_id_type=MESH_ID,
        )
    pl.semaphore_wait(barrier, len(seq_rounds) + dp_count - 1)
    for shift in range(1, dp_count):
        label_copy(shift).start()

    size = in_ref.shape[0]
    base = 0
    copies = []
    for index, (axis, bit) in enumerate(plan):
        half = size // 2
        mine = (coords[axis] // bit) % 2
        keep = base + mine * half
        give = base + (1 - mine) * half
        if index == len(seq_rounds):
            for shift in range(1, dp_count):
                label_copy(shift).wait_recv()
            n_one = label_ref[...] + jnp.sum(label_buf[1:], axis=0)
            own = label_ref[...]
            weight = own / n_one - (1.0 - own) / (dp_count - n_one)
            acc[pl.ds(base, size)] = acc[pl.ds(base, size)] * weight[None]
        source = in_ref if index == 0 else acc
        copy = pltpu.make_async_remote_copy(
            src_ref=source.at[pl.ds(give, half)],
            dst_ref=recv[index],
            send_sem=send_sem.at[index],
            recv_sem=recv_sem.at[index],
            device_id=device_of(axis, bit),
            device_id_type=MESH_ID,
        )
        copy.start()
        copy.wait_recv()
        acc[pl.ds(keep, half)] = source[pl.ds(keep, half)] + recv[index][...]
        copies.append(copy)
        base = keep
        size = half
    out_ref[...] = acc[pl.ds(base, 1)]
    for copy in copies:
        copy.wait_send()
    for shift in range(1, dp_count):
        label_copy(shift).wait_send()


def reduce_scatter_blocks(blocks, label):
    dp_count = lax.axis_size("dp")
    seq_count = lax.axis_size("seq")
    plan = _halving_plan(dp_count, seq_count)
    n_blocks, rows, cols = blocks.shape
    recv_shapes = [pltpu.VMEM((n_blocks >> (i + 1), rows, cols), blocks.dtype) for i in range(len(plan))]
    return pl.pallas_call(
        functools.partial(_reduce_scatter_kernel, plan),
        out_shape=jax.ShapeDtypeStruct((1, rows, cols), blocks.dtype),
        in_specs=[pl.BlockSpec(memory_space=pltpu.VMEM)] * 2,
        out_specs=pl.BlockSpec(memory_space=pltpu.VMEM),
        scratch_shapes=[
            pltpu.VMEM((n_blocks, rows, cols), blocks.dtype),
            pltpu.VMEM((dp_count, 1, cols), jnp.float32),
            pltpu.SemaphoreType.DMA((dp_count,)),
            pltpu.SemaphoreType.DMA((dp_count,)),
        ] + recv_shapes + [
            pltpu.SemaphoreType.DMA((len(plan),)),
            pltpu.SemaphoreType.DMA((len(plan),)),
        ],
        compiler_params=pltpu.CompilerParams(collective_id=1, has_side_effects=True),
    )(blocks, jnp.broadcast_to(label.astype(jnp.float32), (1, cols)))


def to_halving_order(partial, dp_count, seq_count, rows):
    total_bits = (dp_count * seq_count).bit_length() - 1
    cols = partial.shape[-1]
    view = partial.reshape((2,) * total_bits + (rows, cols))
    order = tuple(range(total_bits - 1, -1, -1)) + (total_bits, total_bits + 1)
    return view.transpose(order).reshape(dp_count * seq_count, rows, cols)


def _chain_kernel(chunk, local_ref, decay_ref, hin_ref, send_buf, send_sem, recv_sem):
    count = lax.axis_size("seq")
    me = lax.axis_index("seq")
    row_id = lax.axis_index("dp")
    has_left = (me + count - 1) // count
    has_right = (2 * count - 2 - me) // count
    left = me - has_left
    right = me + has_right
    pieces = local_ref.shape[0] // chunk

    barrier = pltpu.get_barrier_semaphore()

    @pl.when(has_left == 1)
    def _():
        pl.semaphore_signal(barrier, inc=1, device_id=(row_id, left), device_id_type=MESH_ID)

    @pl.when(has_right == 1)
    def _():
        pl.semaphore_signal(barrier, inc=1, device_id=(row_id, right), device_id_type=MESH_ID)

    pl.semaphore_wait(barrier, has_left + has_right)

    def link(source, piece):
        cols = pl.ds(piece * chunk, chunk)
        return pltpu.make_async_remote_copy(
            src_ref=source.at[cols],
            dst_ref=hin_ref.at[cols],
            send_sem=send_sem.at[piece],
            recv_sem=recv_sem.at[piece],
            device_id=(row_id, right),
            device_id_type=MESH_ID,
        )

    @pl.when(has_left == 0)
    def _():
        hin_ref[...] = jnp.zeros_like(hin_ref)
        for piece in range(pieces):
            link(local_ref, piece).start()

    @pl.when(has_left == 1)
    def _():
        for piece in range(pieces):
            cols = pl.ds(piece * chunk, chunk)
            link(send_buf, piece).wait_recv()

            @pl.when(has_right == 1)
            def _():
                send_buf[cols] = decay_ref[...] * hin_ref[cols] + local_ref[cols]
                link(send_buf, piece).start()

    @pl.when(has_right == 1)
    def _():
        for piece in range(pieces):
            link(send_buf, piece).wait_send()


def carry_chain(local_state, decay, pieces=32):
    chunk = local_state.shape[0] // pieces
    return pl.pallas_call(
        functools.partial(_chain_kernel, chunk),
        out_shape=jax.ShapeDtypeStruct(local_state.shape, local_state.dtype),
        in_specs=[pl.BlockSpec(memory_space=pltpu.VMEM)] * 2,
        out_specs=pl.BlockSpec(memory_space=pltpu.VMEM),
        scratch_shapes=[
            pltpu.VMEM(local_state.shape, local_state.dtype),
            pltpu.SemaphoreType.DMA((pieces,)),
            pltpu.SemaphoreType.DMA((pieces,)),
        ],
        compiler_params=pltpu.CompilerParams(collective_id=2, has_side_effects=True),
    )(local_state, decay)


group_heads = 8
highest = lax.Precision.HIGHEST


def from_behind(block, axis, distance):
    devices = range(lax.axis_size(axis))
    route = [(i - distance, i) for i in devices if i - distance in devices]
    return lax.ppermute(block, axis, route)


def state_product(weight, x_wide, b_wide):
    row_count = x_wide.shape[0]
    return lax.dot_general(
        b_wide,
        (weight[:, :, None] * x_wide).reshape(row_count, H * P_SIZE),
        (((0,), (0,)), ((), ())),
        precision=lax.Precision.HIGH,
    )


def local_terms(x_vals, b_vals, c_vals, dt_vals, cumulative, points, offset):
    row_count = x_vals.shape[0]
    x_wide = x_vals.astype(jnp.float32).reshape(row_count, H, P_SIZE)
    b_wide = b_vals.astype(jnp.float32)
    c_wide = c_vals.astype(jnp.float32)
    scores = lax.dot_general(
        c_vals, b_vals, (((1,), (1,)), ((), ())), preferred_element_type=jnp.float32
    )
    positions = jnp.arange(row_count, dtype=jnp.int32)
    causal = positions[:, None] >= positions[None, :]
    masked_scores = jnp.where(causal, scores, 0.0)
    grow = jnp.exp(-cumulative) * dt_vals
    shrink = jnp.exp(cumulative)
    scaled_x = (grow[:, :, None] * x_wide).reshape(row_count, H * P_SIZE)
    mixed = jnp.dot(masked_scores, scaled_x, precision=lax.Precision.HIGH).reshape(row_count, H, P_SIZE)
    diagonal_part = shrink[:, :, None] * mixed
    final_log = cumulative[row_count - 1]
    to_end = jnp.exp(final_log[None, :] - cumulative) * dt_vals
    decay_total = jnp.exp(final_log)
    local_state = state_product(to_end, x_wide, b_wide)
    local_index = points - offset
    owned_flag = ((local_index >= 0) & (local_index < row_count)).astype(jnp.float32)
    one_hot = (positions[None, :] == local_index[:, None]).astype(jnp.float32)
    cum_at = jnp.dot(one_hot, cumulative, precision=highest)
    before = positions[None, :] <= local_index[:, None]
    spread = jnp.where(before[:, :, None], cum_at[:, None, :] - cumulative[None], -1e30)
    read_weight = jnp.sum(owned_flag[:, None, None] * jnp.exp(spread), axis=0) * dt_vals / R
    carry_weight = jnp.sum(owned_flag[:, None] * jnp.exp(cum_at), axis=0) / R
    return (
        diagonal_part, x_wide, b_wide, c_wide, local_state, decay_total, to_end, read_weight, carry_weight
    )


def finish_block(diagonal_part, x_wide, c_wide, cumulative, h_in, gate_rows, d_skip, norm_gain):
    row_count = x_wide.shape[0]
    incoming = jnp.dot(c_wide, h_in, precision=lax.Precision.HIGH).reshape(row_count, H, P_SIZE)
    ssm_out = (
        diagonal_part + jnp.exp(cumulative)[:, :, None] * incoming + d_skip[None, :, None] * x_wide
    )
    gated_out = ssm_out.reshape(row_count, H * P_SIZE) * jax.nn.silu(gate_rows.astype(jnp.float32))
    inv_rms = lax.rsqrt(jnp.mean(gated_out * gated_out, axis=-1, keepdims=True) + 1e-05)
    return (gated_out * inv_rms * norm_gain).astype(jnp.bfloat16)


def on_device(
    xbc,
    gate_input,
    dt_raw,
    conv_weight,
    conv_bias,
    dt_bias,
    a_rate,
    d_skip,
    norm_gain,
    labels,
    readout,
):
    row_count = xbc.shape[1]
    seq_count = lax.axis_size("seq")
    me = lax.axis_index("seq")
    edge_rows = from_behind(xbc[:, row_count - (KW - 1) :, :], "seq", 1)
    padded = jnp.concatenate([edge_rows, xbc], axis=1)[0].astype(jnp.float32)
    conv_sum = conv_bias
    for tap_index in range(KW):
        conv_sum = conv_sum + conv_weight[tap_index] * padded[tap_index : tap_index + row_count]
    activated = jax.nn.silu(conv_sum).astype(jnp.bfloat16)
    dt_vals = jax.nn.softplus(dt_raw[0].astype(jnp.float32) + dt_bias)
    cumulative = jnp.cumsum(-a_rate * dt_vals, axis=0)
    offset = me * row_count
    (diagonal_part, x_wide, b_wide, c_wide, local_state, decay_total, to_end, read_weight,
     carry_weight) = local_terms(
        activated[:, : H * P_SIZE],
        activated[:, H * P_SIZE : H * P_SIZE + N],
        activated[:, H * P_SIZE + N :],
        dt_vals,
        cumulative,
        readout[0],
        offset,
    )
    h_in = carry_chain(local_state, jnp.repeat(decay_total, P_SIZE)[None])
    read_local = state_product(read_weight, x_wide, b_wide)
    mean_state = (jnp.repeat(carry_weight, P_SIZE)[None] * h_in + read_local).T
    batch_count = lax.axis_size("dp")
    block_rows = mean_state.shape[0] // (batch_count * seq_count)
    blocks = to_halving_order(mean_state, batch_count, seq_count, block_rows)
    steering = reduce_scatter_blocks(blocks, labels[0])[0]
    layer_out = finish_block(
        diagonal_part, x_wide, c_wide, cumulative, h_in, gate_input[0], d_skip, norm_gain
    )
    return (layer_out[None], steering)


def solution(mesh):
    return jax.shard_map(
        on_device,
        mesh=mesh,
        in_specs=(
            P("dp", "seq", None),
            P("dp", "seq", None),
            P("dp", "seq", None),
            P(),
            P(),
            P(),
            P(),
            P(),
            P(),
            P("dp"),
            P("dp", None),
        ),
        out_specs=(P("dp", "seq", None), P(("dp", "seq"), None)),
        check_vma=False,
    )
```

```python
import jax
import jax.numpy as jnp
from jax import lax
from jax.sharding import PartitionSpec as P
from jax.experimental import pallas as pl
from jax.experimental.pallas import tpu as pltpu
import functools

H = 40
P_SIZE = 64
N = 128
KW = 4
R = 4


MESH_ID = pl.DeviceIdType.MESH


def _halving_plan(dp_count, seq_count):
    plan = []
    bit = 1
    while bit < seq_count:
        plan.append(("seq", bit))
        bit *= 2
    bit = 1
    while bit < dp_count:
        plan.append(("dp", bit))
        bit *= 2
    return plan


def _reduce_scatter_kernel(plan, in_ref, label_ref, out_ref, acc, label_buf, label_send, label_recv, *rest):
    rounds = len(plan)
    recv = rest[:rounds]
    send_sem, recv_sem = rest[rounds], rest[rounds + 1]
    coords = {"dp": lax.axis_index("dp"), "seq": lax.axis_index("seq")}

    def partner_of(axis, bit):
        me = coords[axis]
        return me + bit - 2 * bit * ((me // bit) % 2)

    def device_of(axis, bit):
        if axis == "dp":
            return (partner_of(axis, bit), coords["seq"])
        return (coords["dp"], partner_of(axis, bit))

    dp_count = lax.axis_size("dp")

    def label_copy(shift):
        return pltpu.make_async_remote_copy(
            src_ref=label_ref,
            dst_ref=label_buf.at[shift],
            send_sem=label_send.at[shift],
            recv_sem=label_recv.at[shift],
            device_id=((coords["dp"] + shift) % dp_count, coords["seq"]),
            device_id_type=MESH_ID,
        )

    barrier = pltpu.get_barrier_semaphore()
    seq_rounds = [(axis, bit) for axis, bit in plan if axis == "seq"]
    for axis, bit in seq_rounds:
        pl.semaphore_signal(barrier, inc=1, device_id=device_of(axis, bit), device_id_type=MESH_ID)
    for shift in range(1, dp_count):
        pl.semaphore_signal(
            barrier, inc=1, device_id=((coords["dp"] + shift) % dp_count, coords["seq"]),
            device_id_type=MESH_ID,
        )
    pl.semaphore_wait(barrier, len(seq_rounds) + dp_count - 1)
    for shift in range(1, dp_count):
        label_copy(shift).start()

    size = in_ref.shape[0]
    base = 0
    copies = []
    for index, (axis, bit) in enumerate(plan):
        half = size // 2
        mine = (coords[axis] // bit) % 2
        keep = base + mine * half
        give = base + (1 - mine) * half
        if index == len(seq_rounds):
            for shift in range(1, dp_count):
                label_copy(shift).wait_recv()
            n_one = label_ref[...] + jnp.sum(label_buf[1:], axis=0)
            own = label_ref[...]
            weight = own / n_one - (1.0 - own) / (dp_count - n_one)
            acc[pl.ds(base, size)] = acc[pl.ds(base, size)] * weight[None]
        source = in_ref if index == 0 else acc
        copy = pltpu.make_async_remote_copy(
            src_ref=source.at[pl.ds(give, half)],
            dst_ref=recv[index],
            send_sem=send_sem.at[index],
            recv_sem=recv_sem.at[index],
            device_id=device_of(axis, bit),
            device_id_type=MESH_ID,
        )
        copy.start()
        copy.wait_recv()
        acc[pl.ds(keep, half)] = source[pl.ds(keep, half)] + recv[index][...]
        copies.append(copy)
        base = keep
        size = half
    out_ref[...] = acc[pl.ds(base, 1)]
    for copy in copies:
        copy.wait_send()
    for shift in range(1, dp_count):
        label_copy(shift).wait_send()


def reduce_scatter_blocks(blocks, label):
    dp_count = lax.axis_size("dp")
    seq_count = lax.axis_size("seq")
    plan = _halving_plan(dp_count, seq_count)
    n_blocks, rows, cols = blocks.shape
    recv_shapes = [pltpu.VMEM((n_blocks >> (i + 1), rows, cols), blocks.dtype) for i in range(len(plan))]
    return pl.pallas_call(
        functools.partial(_reduce_scatter_kernel, plan),
        out_shape=jax.ShapeDtypeStruct((1, rows, cols), blocks.dtype),
        in_specs=[pl.BlockSpec(memory_space=pltpu.VMEM)] * 2,
        out_specs=pl.BlockSpec(memory_space=pltpu.VMEM),
        scratch_shapes=[
            pltpu.VMEM((n_blocks, rows, cols), blocks.dtype),
            pltpu.VMEM((dp_count, 1, cols), jnp.float32),
            pltpu.SemaphoreType.DMA((dp_count,)),
            pltpu.SemaphoreType.DMA((dp_count,)),
        ] + recv_shapes + [
            pltpu.SemaphoreType.DMA((len(plan),)),
            pltpu.SemaphoreType.DMA((len(plan),)),
        ],
        compiler_params=pltpu.CompilerParams(collective_id=1, has_side_effects=True),
    )(blocks, jnp.broadcast_to(label.astype(jnp.float32), (1, cols)))


def to_halving_order(partial, dp_count, seq_count, rows):
    total_bits = (dp_count * seq_count).bit_length() - 1
    cols = partial.shape[-1]
    view = partial.reshape((2,) * total_bits + (rows, cols))
    order = tuple(range(total_bits - 1, -1, -1)) + (total_bits, total_bits + 1)
    return view.transpose(order).reshape(dp_count * seq_count, rows, cols)


def _chain_kernel(chunk, local_ref, decay_ref, hin_ref, send_buf, send_sem, recv_sem):
    count = lax.axis_size("seq")
    me = lax.axis_index("seq")
    row_id = lax.axis_index("dp")
    has_left = (me + count - 1) // count
    has_right = (2 * count - 2 - me) // count
    left = me - has_left
    right = me + has_right
    pieces = local_ref.shape[0] // chunk

    barrier = pltpu.get_barrier_semaphore()

    @pl.when(has_left == 1)
    def _():
        pl.semaphore_signal(barrier, inc=1, device_id=(row_id, left), device_id_type=MESH_ID)

    @pl.when(has_right == 1)
    def _():
        pl.semaphore_signal(barrier, inc=1, device_id=(row_id, right), device_id_type=MESH_ID)

    pl.semaphore_wait(barrier, has_left + has_right)

    def link(source, piece):
        cols = pl.ds(piece * chunk, chunk)
        return pltpu.make_async_remote_copy(
            src_ref=source.at[cols],
            dst_ref=hin_ref.at[cols],
            send_sem=send_sem.at[piece],
            recv_sem=recv_sem.at[piece],
            device_id=(row_id, right),
            device_id_type=MESH_ID,
        )

    @pl.when(has_left == 0)
    def _():
        hin_ref[...] = jnp.zeros_like(hin_ref)
        for piece in range(pieces):
            link(local_ref, piece).start()

    @pl.when(has_left == 1)
    def _():
        for piece in range(pieces):
            cols = pl.ds(piece * chunk, chunk)
            link(send_buf, piece).wait_recv()

            @pl.when(has_right == 1)
            def _():
                send_buf[cols] = decay_ref[...] * hin_ref[cols] + local_ref[cols]
                link(send_buf, piece).start()

    @pl.when(has_right == 1)
    def _():
        for piece in range(pieces):
            link(send_buf, piece).wait_send()


def carry_chain(local_state, decay, pieces=64):
    chunk = local_state.shape[0] // pieces
    return pl.pallas_call(
        functools.partial(_chain_kernel, chunk),
        out_shape=jax.ShapeDtypeStruct(local_state.shape, local_state.dtype),
        in_specs=[pl.BlockSpec(memory_space=pltpu.VMEM)] * 2,
        out_specs=pl.BlockSpec(memory_space=pltpu.VMEM),
        scratch_shapes=[
            pltpu.VMEM(local_state.shape, local_state.dtype),
            pltpu.SemaphoreType.DMA((pieces,)),
            pltpu.SemaphoreType.DMA((pieces,)),
        ],
        compiler_params=pltpu.CompilerParams(collective_id=2, has_side_effects=True),
    )(local_state, decay)


group_heads = 8
highest = lax.Precision.HIGHEST


def from_behind(block, axis, distance):
    devices = range(lax.axis_size(axis))
    route = [(i - distance, i) for i in devices if i - distance in devices]
    return lax.ppermute(block, axis, route)


def state_product(weight, x_wide, b_wide):
    row_count = x_wide.shape[0]
    return lax.dot_general(
        b_wide,
        (weight[:, :, None] * x_wide).reshape(row_count, H * P_SIZE),
        (((0,), (0,)), ((), ())),
        precision=lax.Precision.HIGH,
    )


def local_terms(x_vals, b_vals, c_vals, dt_vals, cumulative, points, offset):
    row_count = x_vals.shape[0]
    x_wide = x_vals.astype(jnp.float32).reshape(row_count, H, P_SIZE)
    b_wide = b_vals.astype(jnp.float32)
    c_wide = c_vals.astype(jnp.float32)
    scores = lax.dot_general(
        c_vals, b_vals, (((1,), (1,)), ((), ())), preferred_element_type=jnp.float32
    )
    positions = jnp.arange(row_count, dtype=jnp.int32)
    causal = positions[:, None] >= positions[None, :]
    masked_scores = jnp.where(causal, scores, 0.0)
    grow = jnp.exp(-cumulative) * dt_vals
    shrink = jnp.exp(cumulative)
    scaled_x = (grow[:, :, None] * x_wide).reshape(row_count, H * P_SIZE)
    mixed = jnp.dot(masked_scores, scaled_x, precision=lax.Precision.HIGH).reshape(row_count, H, P_SIZE)
    diagonal_part = shrink[:, :, None] * mixed
    final_log = cumulative[row_count - 1]
    to_end = jnp.exp(final_log[None, :] - cumulative) * dt_vals
    decay_total = jnp.exp(final_log)
    local_state = state_product(to_end, x_wide, b_wide)
    local_index = points - offset
    owned_flag = ((local_index >= 0) & (local_index < row_count)).astype(jnp.float32)
    one_hot = (positions[None, :] == local_index[:, None]).astype(jnp.float32)
    cum_at = jnp.dot(one_hot, cumulative, precision=highest)
    before = positions[None, :] <= local_index[:, None]
    spread = jnp.where(before[:, :, None], cum_at[:, None, :] - cumulative[None], -1e30)
    read_weight = jnp.sum(owned_flag[:, None, None] * jnp.exp(spread), axis=0) * dt_vals / R
    carry_weight = jnp.sum(owned_flag[:, None] * jnp.exp(cum_at), axis=0) / R
    return (
        diagonal_part, x_wide, b_wide, c_wide, local_state, decay_total, to_end, read_weight, carry_weight
    )


def finish_block(diagonal_part, x_wide, c_wide, cumulative, h_in, gate_rows, d_skip, norm_gain):
    row_count = x_wide.shape[0]
    incoming = jnp.dot(c_wide, h_in, precision=lax.Precision.HIGH).reshape(row_count, H, P_SIZE)
    ssm_out = (
        diagonal_part + jnp.exp(cumulative)[:, :, None] * incoming + d_skip[None, :, None] * x_wide
    )
    gated_out = ssm_out.reshape(row_count, H * P_SIZE) * jax.nn.silu(gate_rows.astype(jnp.float32))
    inv_rms = lax.rsqrt(jnp.mean(gated_out * gated_out, axis=-1, keepdims=True) + 1e-05)
    return (gated_out * inv_rms * norm_gain).astype(jnp.bfloat16)


def on_device(
    xbc,
    gate_input,
    dt_raw,
    conv_weight,
    conv_bias,
    dt_bias,
    a_rate,
    d_skip,
    norm_gain,
    labels,
    readout,
):
    row_count = xbc.shape[1]
    seq_count = lax.axis_size("seq")
    me = lax.axis_index("seq")
    edge_rows = from_behind(xbc[:, row_count - (KW - 1) :, :], "seq", 1)
    padded = jnp.concatenate([edge_rows, xbc], axis=1)[0].astype(jnp.float32)
    conv_sum = conv_bias
    for tap_index in range(KW):
        conv_sum = conv_sum + conv_weight[tap_index] * padded[tap_index : tap_index + row_count]
    activated = jax.nn.silu(conv_sum).astype(jnp.bfloat16)
    dt_vals = jax.nn.softplus(dt_raw[0].astype(jnp.float32) + dt_bias)
    cumulative = jnp.cumsum(-a_rate * dt_vals, axis=0)
    offset = me * row_count
    (diagonal_part, x_wide, b_wide, c_wide, local_state, decay_total, to_end, read_weight,
     carry_weight) = local_terms(
        activated[:, : H * P_SIZE],
        activated[:, H * P_SIZE : H * P_SIZE + N],
        activated[:, H * P_SIZE + N :],
        dt_vals,
        cumulative,
        readout[0],
        offset,
    )
    h_in = carry_chain(local_state, jnp.repeat(decay_total, P_SIZE)[None])
    read_local = state_product(read_weight, x_wide, b_wide)
    mean_state = (jnp.repeat(carry_weight, P_SIZE)[None] * h_in + read_local).T
    batch_count = lax.axis_size("dp")
    block_rows = mean_state.shape[0] // (batch_count * seq_count)
    blocks = to_halving_order(mean_state, batch_count, seq_count, block_rows)
    steering = reduce_scatter_blocks(blocks, labels[0])[0]
    layer_out = finish_block(
        diagonal_part, x_wide, c_wide, cumulative, h_in, gate_input[0], d_skip, norm_gain
    )
    return (layer_out[None], steering)


def solution(mesh):
    return jax.shard_map(
        on_device,
        mesh=mesh,
        in_specs=(
            P("dp", "seq", None),
            P("dp", "seq", None),
            P("dp", "seq", None),
            P(),
            P(),
            P(),
            P(),
            P(),
            P(),
            P("dp"),
            P("dp", None),
        ),
        out_specs=(P("dp", "seq", None), P(("dp", "seq"), None)),
        check_vma=False,
    )
```
